256 devices in a mesh: slab: 4 (over y), freq: 64 (over z, x, core).
Axes of the slice: x: 4, y: 4, z: 8, core: 2. Of those that a mesh axis runs over, the one named last changes fastest.
Arguments:
- initial: float32 [2, 512, 128, 256], P(None, 'freq', 'slab'), may hold values from -6 to 6
- measured: float32 [2, 512, 128, 256], P(None, 'freq', 'slab'), may hold values from -6 to 6
- projector: bfloat16 [3, 2, 512, 256, 256], P(None, None, 'freq'), may hold values from -0.15625 to 0.15625
- offsets: int32 [3], replicated, may hold values from -16 to 16, as said below
Outputs:
- volume: float32 [128, 256, 1024], P('slab', 'freq')
The draws below stay inside these ranges and needn't reach their ends.
Inputs may be any that keep to these rules, and one draw needn't show every extreme that they name: `offsets`: the first entry is +16 or -16; the third is its negative; the second lies strictly between -16 and 16.
All inputs are finite; a program needn't handle non-finite values.
Results may differ from the reference program's by a relative error of at most 0.005.
Values may be sent and summed in bfloat16 or wider, within the bound.
No kernel may reach another device: no remote copies, remote signals or barrier semaphores. Data moves between devices by JAX's collectives and lax.ppermute only.
A program may use at most 128 MiB of HBM per device.

```python
import math
import jax
import jax.numpy as jnp
from jax import lax

A = 1024
R = 256
U = 256
HALO = 16
INNER = 2
OUTER = 2
K = 512
Z = 128


def draw_offsets(key, part):
    first_key, second_key = jax.random.split(jax.random.fold_in(key, 7), 2)
    signum = 2 * jax.random.randint(first_key, (), 0, 2) - 1
    middle = jax.random.randint(second_key, (), -HALO + 1, HALO)
    return jnp.stack([signum * HALO, middle, -signum * HALO]).astype(jnp.int32)


def shard_levels(key, dims, pieces, low, high):
    def one(dim, shards_of):
        draws = jax.random.uniform(jax.random.fold_in(jax.random.fold_in(key, 6), dim), (shards_of,), jnp.float32, low / len(pieces), high / len(pieces))
        return jnp.repeat(jnp.exp(draws), dims[dim] // shards_of).reshape((-1,) + (1,) * (len(dims) - dim - 1))

    level = one(*pieces[0])
    for cut in pieces[1:]:
        level = level * one(*cut)
    return level


def gaussian(stream_key, shape, scale, limit, cuts=(), kind=jnp.bfloat16):
    array = scale * jax.random.normal(stream_key, shape, jnp.float32)
    if cuts:
        array = array * shard_levels(stream_key, shape, cuts, -0.22, 0.18)
    return jnp.clip(array, -limit, limit).astype(kind)


def setup_inputs(seed: int = 0) -> dict:
    keys = jax.random.split(jax.random.key(seed), 5)
    return {
        "initial": gaussian(keys[0], (2, K, Z, R), 1.0, 6.0, ((1, 64), (2, 4)), jnp.float32),
        "measured": gaussian(keys[1], (2, K, Z, U), 1.0, 6.0, ((1, 64), (2, 4)), jnp.float32),
        "projector": gaussian(keys[2], (3, 2, K, R, U), (6 * R) ** -0.5, 0.15625, ((2, 64),)),
        "offsets": draw_offsets(jax.random.fold_in(keys[4], 71), 0),
    }


STEP_SIZE = 0.25
CLIP_LEVEL = 1.0
SMOOTHING = 0.25

def angle_tables():
    frequency = jnp.arange(A // 2, dtype=jnp.int32)[:, None]
    angles = jnp.arange(A, dtype=jnp.int32)[None, :]
    phases = (frequency * angles % A).astype(jnp.float32) * (2.0 * math.pi / A)
    cosine = jnp.cos(phases)
    sines = jnp.sin(phases)
    weights = jnp.where(frequency == 0, 1.0, 2.0).astype(jnp.float32)
    factor = 1.0 / math.sqrt(A)
    synthesis = jnp.stack([weights * cosine, -weights * sines]) * factor
    analysis = jnp.stack([cosine, -sines]) * factor
    return (synthesis, analysis)

def shrink(volume):
    forward_diff = jnp.roll(volume, -1, axis=2) - volume
    clipped = jnp.clip(forward_diff, -CLIP_LEVEL, CLIP_LEVEL)
    return volume - SMOOTHING * (jnp.roll(clipped, 1, axis=2) - clipped)

def contract(left, right, form):
    return jnp.einsum(form, left.astype(jnp.float32), right.astype(jnp.float32), precision=lax.Precision.HIGHEST)

def project(rounded, projector, offsets):
    slices = rounded.shape[2]
    padded = jnp.pad(rounded, ((0, 0), (0, 0), (HALO, HALO), (0, 0)))
    sum_real = 0.0
    sum_imag = 0.0
    for slot in range(3):
        shifted = lax.dynamic_slice_in_dim(padded, (HALO + offsets[slot]).astype(jnp.int32), slices, 2)
        real_weight = projector[slot, 0]
        imag_weight = projector[slot, 1]
        sum_real = sum_real + contract(shifted[0], real_weight, 'kzr,kru->kzu') - contract(shifted[1], imag_weight, 'kzr,kru->kzu')
        sum_imag = sum_imag + contract(shifted[0], imag_weight, 'kzr,kru->kzu') + contract(shifted[1], real_weight, 'kzr,kru->kzu')
    return jnp.stack([sum_real, sum_imag])

def back_project(residual, projector, offsets):
    slices = residual.shape[2]
    padded = jnp.pad(residual, ((0, 0), (0, 0), (HALO, HALO), (0, 0)))
    sum_real = 0.0
    sum_imag = 0.0
    for slot in range(3):
        shifted = lax.dynamic_slice_in_dim(padded, (HALO - offsets[slot]).astype(jnp.int32), slices, 2)
        real_weight = projector[slot, 0]
        imag_weight = projector[slot, 1]
        sum_real = sum_real + contract(shifted[0], real_weight, 'kzu,kru->kzr') + contract(shifted[1], imag_weight, 'kzu,kru->kzr')
        sum_imag = sum_imag + contract(shifted[1], real_weight, 'kzu,kru->kzr') - contract(shifted[0], imag_weight, 'kzu,kru->kzr')
    return jnp.stack([sum_real, sum_imag])

def reference(initial, measured, projector, offsets):
    synthesis, analysis = angle_tables()
    iterate = initial
    volume = None
    for outer_step in range(OUTER):
        for inner_step in range(INNER):
            rounded = iterate.astype(jnp.bfloat16)
            projected = project(rounded, projector, offsets)
            residual = (measured - projected).astype(jnp.bfloat16)
            iterate = iterate + STEP_SIZE * back_project(residual, projector, offsets)
        volume = contract(iterate, synthesis, 'pkzr,pka->zra')
        volume = shrink(volume)
        if outer_step + 1 < OUTER:
            iterate = contract(volume, analysis, 'zra,pka->pkzr')
    return volume
```

```python
import math

import jax
import jax.numpy as jnp
import numpy as np
from jax import lax
from jax.experimental import pallas as pl
from jax.experimental.pallas import tpu as pltpu
from jax.sharding import PartitionSpec as P

A = 1024
Q = A // 4
STEP_SIZE = 0.25
CLIP_LEVEL = 1.0
SMOOTHING = 0.25
INNER = 2
SLABS = 4
GROUPS = 64
Z = 128
R = 256
F32 = jnp.float32
BF16 = jnp.bfloat16
SEND_INPUT = jnp.float16
SEND_OUT = (BF16, F32)
SEND_BACK = BF16
VMEM = pl.BlockSpec(memory_space=pltpu.VMEM)
SMEM = pl.BlockSpec(memory_space=pltpu.SMEM)
ANY = pl.BlockSpec(memory_space=pl.ANY)


def split_table(table):
    high = table.astype(np.float32).astype(jnp.bfloat16)
    low = (table - high.astype(np.float64)).astype(np.float32).astype(jnp.bfloat16)
    return high, low


def tables():
    group, half, part = np.meshgrid(np.arange(GROUPS), np.arange(2), np.arange(2), indexing="ij")
    plain, turned, weights = [], [], []
    for residue in range(4):
        k = (8 * group + residue + 4 * half).reshape(-1)
        imag = part.reshape(-1)[:, None] == 1
        phase = (k[:, None] * np.arange(Q)[None, :] % A) * (2.0 * math.pi / A)
        plain.append(np.where(imag, -np.sin(phase), np.cos(phase)) / math.sqrt(A))
        turned.append(np.where(imag, -np.cos(phase), -np.sin(phase)) / math.sqrt(A))
        weights.append(np.where(k == 0, 1.0, 2.0)[:, None])
    synth = [(p * w).T for p, w in zip(plain, weights)]
    synth_turned = [(t * w).T for t, w in zip(turned, weights)]
    to_angles = np.concatenate(
        [synth[0], synth[2], synth[1], synth_turned[1], synth[3], synth_turned[3]], axis=0
    )
    even = np.concatenate([plain[0], plain[2]], axis=0)
    odd = np.concatenate(
        [np.concatenate([plain[c], turned[c]], axis=1) for c in (1, 3)], axis=0
    )
    return split_table(to_angles), split_table(even), split_table(odd)


def dot(left, right):
    return jnp.dot(left, right, preferred_element_type=F32)


def prepare_kernel(slab_ref, projector_ref, plain_ref, turned_ref, sems):
    slab = slab_ref[0]
    copies = []
    for half in range(2):
        for part in range(2):
            for slot in range(3):
                copy = pltpu.make_async_copy(
                    projector_ref.at[slot, part, slab + 4 * half],
                    plain_ref.at[half, part, :, pl.ds(R * slot, R)],
                    sems.at[len(copies)],
                )
                copy.start()
                copies.append(copy)
    index = 0
    for half in range(2):
        for part in range(2):
            for slot in range(3):
                copies[index].wait()
                index += 1
                cols = pl.ds(R * slot, R)
                turned_ref[half, part, :, cols] = plain_ref[half, part, :, cols].T


def prepare(slab, projector):
    shape = jax.ShapeDtypeStruct((2, 2, R, 3 * R), BF16)
    return pl.pallas_call(
        prepare_kernel,
        out_shape=(shape, shape),
        in_specs=[SMEM, ANY],
        out_specs=(VMEM, VMEM),
        scratch_shapes=[pltpu.SemaphoreType.DMA((12,))],
        cost_estimate=pl.CostEstimate(flops=0, bytes_accessed=8 << 20, transcendentals=0),
        name="prepare",
    )(slab, projector)


def moved(values, offset, lane):
    source = lane + offset
    rolled = pltpu.roll(values, lax.rem(Z - offset, Z), 1)
    return jnp.where((source >= 0) & (source < Z), rolled, 0.0).astype(BF16)


def swap_blocks(blocks):
    lane = lax.broadcasted_iota(jnp.int32, blocks[0].shape, 1)
    odd32 = (lane // 32) % 2 == 1
    high64 = lane >= 64
    a, b, c, d = blocks
    for_pairs = []
    for low, high in ((a, b), (c, d)):
        for_pairs.append(
            (
                jnp.where(odd32, pltpu.roll(high, 32, 1), low),
                jnp.where(odd32, high, pltpu.roll(low, 96, 1)),
            )
        )
    (a, b), (c, d) = for_pairs
    out = [None] * 4
    for i, (low, high) in enumerate(((a, c), (b, d))):
        out[i] = jnp.where(high64, pltpu.roll(high, 64, 1), low)
        out[i + 2] = jnp.where(high64, high, pltpu.roll(low, 64, 1))
    return out


def passes(offsets_ref, plain_ref, turned_ref, iterate, measured, shifted):
    lane = lax.broadcasted_iota(jnp.int32, (R, Z), 1)

    def step(count, carry):
        half = lax.rem(count, 2)
        for slot in range(3):
            rows = pl.ds(R * slot, R)
            offset = offsets_ref[slot]
            shifted[rows, :Z] = moved(iterate[half, 0], offset, lane)
            shifted[rows, Z:] = moved(iterate[half, 1], offset, lane)
        by_real = dot(turned_ref[half, 0], shifted[...])
        by_imag = dot(turned_ref[half, 1], shifted[...])
        real = measured[half, 0] - (by_real[:, :Z] - by_imag[:, Z:])
        imag = measured[half, 1] - (by_imag[:, :Z] + by_real[:, Z:])
        real = real.astype(BF16).astype(F32)
        imag = imag.astype(BF16).astype(F32)
        for slot in range(3):
            rows = pl.ds(R * slot, R)
            offset = -offsets_ref[slot]
            shifted[rows, :Z] = moved(real, offset, lane)
            shifted[rows, Z:] = moved(imag, offset, lane)
        by_real = dot(plain_ref[half, 0], shifted[...])
        by_imag = dot(plain_ref[half, 1], shifted[...])
        iterate[half, 0] += STEP_SIZE * (by_real[:, :Z] + by_imag[:, Z:])
        iterate[half, 1] += STEP_SIZE * (by_real[:, Z:] - by_imag[:, :Z])
        return carry

    lax.fori_loop(0, 2 * INNER, step, 0)


def pack(iterate, rows_ref, packed_ref):
    for half in range(2):
        for part in range(2):
            blocks = [iterate[half, part, pl.ds(i, GROUPS, stride=4), :] for i in range(4)]
            for slab, block in enumerate(swap_blocks(blocks)):
                rows_ref[pl.ds(Q * slab + 2 * half + part, GROUPS, stride=4), :] = block
    packed_ref[...] = rows_ref[...].astype(packed_ref.dtype)


def first_kernel(
    slab_ref, offsets_ref, own, one, two, three, plain_ref, turned_ref,
    packed_ref, measured_out, column, iterate, shifted, rows_ref,
):
    slab = slab_ref[0]
    for array, target in ((0, iterate), (1, measured_out)):
        for half in range(2):
            for part in range(2):
                for distance, piece in enumerate((own, one, two, three)):
                    start = 32 * lax.rem(slab + 4 - distance, 4)
                    column[pl.ds(pl.multiple_of(start, 32), 32), :] = piece[array, part, half].astype(F32)
                target[half, part] = column[...].T
    passes(offsets_ref, plain_ref, turned_ref, iterate, measured_out, shifted)
    pack(iterate, rows_ref, packed_ref)


def second_kernel(
    offsets_ref, packed_in, measured_ref, plain_ref, turned_ref,
    packed_ref, iterate, shifted, rows_ref,
):
    rows_ref[...] = packed_in[...].astype(F32)
    for half in range(2):
        for part in range(2):
            blocks = [
                rows_ref[pl.ds(Q * slab + 2 * half + part, GROUPS, stride=4), :] for slab in range(4)
            ]
            for i, block in enumerate(swap_blocks(blocks)):
                iterate[half, part, pl.ds(i, GROUPS, stride=4), :] = block
    passes(offsets_ref, plain_ref, turned_ref, iterate, measured_ref, shifted)
    pack(iterate, rows_ref, packed_ref)


def pass_scratch():
    return [
        pltpu.VMEM((2, 2, R, Z), F32),
        pltpu.VMEM((3 * R, 2 * Z), BF16),
        pltpu.VMEM((4 * Q, Z), F32),
    ]


PASS_COST = pl.CostEstimate(flops=2 << 30, bytes_accessed=8 << 20, transcendentals=0)


def first_half(slab, offsets, pieces, plain, turned, send_type):
    return pl.pallas_call(
        first_kernel,
        out_shape=(
            jax.ShapeDtypeStruct((4 * Q, Z), send_type),
            jax.ShapeDtypeStruct((2, 2, R, Z), F32),
        ),
        in_specs=[SMEM, SMEM] + [VMEM] * 6,
        out_specs=(VMEM, VMEM),
        scratch_shapes=[pltpu.VMEM((Z, R), F32)] + pass_scratch(),
        cost_estimate=PASS_COST,
        name="first_half",
    )(slab, offsets, *pieces, plain, turned)


def later_half(offsets, packed, measured, plain, turned, send_type):
    return pl.pallas_call(
        second_kernel,
        out_shape=jax.ShapeDtypeStruct((4 * Q, Z), send_type),
        in_specs=[SMEM] + [VMEM] * 4,
        out_specs=VMEM,
        scratch_shapes=pass_scratch(),
        cost_estimate=PASS_COST,
        name="later_half",
    )(offsets, packed, measured, plain, turned)


def to_volume(packed_ref, high_ref, low_ref, volume):
    def residue(c, rows):
        block = packed_ref[pl.ds(Q * c, Q), :]
        if block.dtype == BF16:
            return dot(high_ref[rows, :], block) + dot(low_ref[rows, :], block)
        high = block.astype(BF16)
        low = (block - high.astype(F32)).astype(BF16)
        both = dot(high_ref[rows, :], jnp.concatenate([high, low], axis=1))
        return both[:, :Z] + both[:, Z:] + dot(low_ref[rows, :], high)

    zero = residue(0, pl.ds(0, Q))
    two = residue(2, pl.ds(Q, Q))
    same, other = zero + two, zero - two
    one = residue(1, pl.ds(2 * Q, 2 * Q))
    three = residue(3, pl.ds(4 * Q, 2 * Q))
    plain = one[:Q] + three[:Q]
    turned = one[Q:] - three[Q:]
    volume[pl.ds(8, Q), :] = same + plain
    volume[pl.ds(8 + Q, Q), :] = other + turned
    volume[pl.ds(8 + 2 * Q, Q), :] = same - plain
    volume[pl.ds(8 + 3 * Q, Q), :] = other - turned
    volume[7:8, :] = volume[A + 7 : A + 8, :]
    volume[A + 8 : A + 9, :] = volume[8:9, :]


def smooth(volume, start):
    here = volume[pl.ds(8 + start, Q), :]
    before = volume[pl.ds(7 + start, Q), :]
    after = volume[pl.ds(9 + start, Q), :]
    ahead = jnp.clip(after - here, -CLIP_LEVEL, CLIP_LEVEL)
    behind = jnp.clip(here - before, -CLIP_LEVEL, CLIP_LEVEL)
    return here - SMOOTHING * (behind - ahead)


def split(values):
    high = values.astype(BF16)
    return high, (values - high.astype(F32)).astype(BF16)


def wide_dot(high_table, low_table, values):
    high, low = split(values)
    both = dot(high_table, jnp.concatenate([high, low], axis=1))
    return both[:, :Z] + both[:, Z:] + dot(low_table, high)


def middle_kernel(
    packed_ref, high_ref, low_ref, even_high, even_low, odd_high, odd_low, spectra_ref, volume
):
    to_volume(packed_ref, high_ref, low_ref, volume)
    quarters = [smooth(volume, Q * m) for m in range(4)]
    same, cross = quarters[0] + quarters[2], quarters[1] + quarters[3]
    plain, turned = quarters[0] - quarters[2], quarters[1] - quarters[3]

    def put(c, values):
        spectra_ref[pl.ds(Q * c, Q), :] = values.astype(spectra_ref.dtype)

    put(0, wide_dot(even_high[:Q], even_low[:Q], same + cross))
    put(2, wide_dot(even_high[Q:], even_low[Q:], same - cross))
    put(1, wide_dot(odd_high[:Q], odd_low[:Q], jnp.concatenate([plain, turned], axis=0)))
    put(3, wide_dot(odd_high[Q:], odd_low[Q:], jnp.concatenate([plain, -turned], axis=0)))


def middle(packed, angles, even, odd):
    return pl.pallas_call(
        middle_kernel,
        out_shape=jax.ShapeDtypeStruct((4 * Q, Z), SEND_BACK),
        in_specs=[VMEM] * 7,
        out_specs=VMEM,
        scratch_shapes=[pltpu.VMEM((A + 16, Z), F32)],
        cost_estimate=pl.CostEstimate(flops=1 << 30, bytes_accessed=4 << 20, transcendentals=0),
        name="middle",
    )(packed, *angles, *even, *odd)


def last_kernel(packed_ref, high_ref, low_ref, out_ref, volume):
    to_volume(packed_ref, high_ref, low_ref, volume)
    for m in range(4):
        values = smooth(volume, Q * m).T
        for i in range(4):
            out_ref[:, i, pl.ds(Q * m, Q)] = values[32 * i : 32 * (i + 1), :]


def last(packed, angles):
    return pl.pallas_call(
        last_kernel,
        out_shape=jax.ShapeDtypeStruct((Z // SLABS, R // GROUPS, A), F32),
        in_specs=[VMEM] * 3,
        out_specs=VMEM,
        scratch_shapes=[pltpu.VMEM((A + 16, Z), F32)],
        cost_estimate=pl.CostEstimate(flops=1 << 29, bytes_accessed=4 << 20, transcendentals=0),
        name="last",
    )(packed, *angles)


def exchange(packed):
    blocks = packed.reshape(SLABS * GROUPS, 4, Z)
    return lax.all_to_all(blocks, ("slab", "freq"), 0, 0, tiled=True).reshape(packed.shape)


def on_device(initial, measured, projector, offsets):
    angles, even, odd = tables()
    slab = lax.axis_index("slab").astype(jnp.int32)
    both = jnp.stack([initial, measured]).astype(SEND_INPUT)
    both = both.reshape(2, 2, 2, SLABS, *initial.shape[2:])
    pieces = []
    for distance in range(SLABS):
        piece = lax.dynamic_index_in_dim(both, lax.rem(slab + distance, SLABS), 3, keepdims=False)
        if distance:
            piece = lax.ppermute(piece, "slab", [(i, (i + distance) % SLABS) for i in range(SLABS)])
        pieces.append(piece.astype(F32))
    slab = slab.reshape(1)
    plain, turned = prepare(slab, projector)
    packed, measured = first_half(slab, offsets, pieces, plain, turned, SEND_OUT[0])
    packed = exchange(middle(exchange(packed), angles, even, odd))
    packed = later_half(offsets, packed, measured, plain, turned, SEND_OUT[1])
    return last(exchange(packed), angles)


def solution(mesh):
    placed = (
        P(None, "freq", "slab", None),
        P(None, "freq", "slab", None),
        P(None, None, "freq", None, None),
        P(),
    )
    return jax.shard_map(
        on_device, mesh=mesh, in_specs=placed, out_specs=P("slab", "freq", None), check_vma=False
    )
```

```python
import math

import jax
import jax.numpy as jnp
import numpy as np
from jax import lax
from jax.experimental import pallas as pl
from jax.experimental.pallas import tpu as pltpu
from jax.sharding import PartitionSpec as P

A = 1024
Q = A // 4
STEP_SIZE = 0.25
CLIP_LEVEL = 1.0
SMOOTHING = 0.25
INNER = 2
SLABS = 4
GROUPS = 64
Z = 128
R = 256
F32 = jnp.float32
BF16 = jnp.bfloat16
LEVELS = 32000.0
VMEM = pl.BlockSpec(memory_space=pltpu.VMEM)
SMEM = pl.BlockSpec(memory_space=pltpu.SMEM)
HBM = pl.BlockSpec(memory_space=pltpu.HBM)


def split_table(table):
    high = table.astype(np.float32).astype(jnp.bfloat16)
    low = (table - high.astype(np.float64)).astype(np.float32).astype(jnp.bfloat16)
    return high, low


def tables():
    group, half, part = np.meshgrid(np.arange(GROUPS), np.arange(2), np.arange(2), indexing="ij")
    plain, turned, weights = [], [], []
    for residue in range(4):
        k = (8 * group + residue + 4 * half).reshape(-1)
        imag = part.reshape(-1)[:, None] == 1
        phase = (k[:, None] * np.arange(Q)[None, :] % A) * (2.0 * math.pi / A)
        plain.append(np.where(imag, -np.sin(phase), np.cos(phase)) / math.sqrt(A))
        turned.append(np.where(imag, -np.cos(phase), -np.sin(phase)) / math.sqrt(A))
        weights.append(np.where(k == 0, 1.0, 2.0)[:, None])
    synth = [(p * w).T for p, w in zip(plain, weights)]
    synth_turned = [(t * w).T for t, w in zip(turned, weights)]
    to_angles = np.concatenate(
        [synth[0], synth[2], synth[1], synth_turned[1], synth[3], synth_turned[3]], axis=0
    )
    even = np.concatenate([plain[0], plain[2]], axis=0)
    odd = np.concatenate(
        [np.concatenate([plain[c], turned[c]], axis=1) for c in (1, 3)], axis=0
    )
    return split_table(to_angles), split_table(even), split_table(odd)


def cost(flops, size):
    return pl.CostEstimate(flops=flops, bytes_accessed=size, transcendentals=0)


PARAMS = pltpu.CompilerParams(vmem_limit_bytes=20 << 20)
ALONE = pltpu.CompilerParams(vmem_limit_bytes=100 << 19)
SPECTRUM = jax.ShapeDtypeStruct((2, R, Z), F32)
PACKED = jax.ShapeDtypeStruct((4 * Q, Z), BF16)


def dot(left, right):
    return jnp.dot(left, right, preferred_element_type=F32)


def prepare_kernel(slab_ref, projector_ref, blocks_ref, blocks, sems):
    slab = slab_ref[0]
    loads, stores = [], []
    for half in range(2):
        for part in range(2):
            for slot in range(3):
                copy = pltpu.make_async_copy(
                    projector_ref.at[slot, part, slab + 4 * half],
                    blocks.at[half, 2 + part, :, pl.ds(R * slot, R)],
                    sems.at[len(loads)],
                )
                copy.start()
                loads.append(copy)
    for half in range(2):
        for part in range(2):
            for slot in range(3):
                loads[6 * half + 3 * part + slot].wait()
                cols = pl.ds(R * slot, R)
                blocks[half, part, :, cols] = blocks[half, 2 + part, :, cols].T
        copy = pltpu.make_async_copy(blocks.at[half], blocks_ref.at[half], sems.at[12 + half])
        copy.start()
        stores.append(copy)
    for copy in stores:
        copy.wait()


def prepare(slab, projector):
    return pl.pallas_call(
        prepare_kernel,
        out_shape=jax.ShapeDtypeStruct((4, 4, R, 3 * R), BF16),
        in_specs=[SMEM, HBM],
        out_specs=HBM,
        scratch_shapes=[pltpu.VMEM((2, 4, R, 3 * R), BF16), pltpu.SemaphoreType.DMA((14,))],
        compiler_params=ALONE,
        cost_estimate=cost(0, 8 << 20),
        name="prepare",
    )(slab, projector)


def encode(values):
    largest = jnp.max(jnp.max(jnp.abs(values), axis=1, keepdims=True), axis=0, keepdims=True)
    power = jnp.clip(jnp.ceil(jnp.log2(largest)), -100.0, 100.0)
    return jnp.round(values * (LEVELS * jnp.exp2(-power))).astype(jnp.int32), power


def arrange_kernel(slab_ref, initial_ref, measured_ref, own_ref, *piece_refs):
    slab = slab_ref[0]
    row = lax.broadcasted_iota(jnp.int32, (16, Z), 0)
    for array, source in enumerate((initial_ref, measured_ref)):
        for part in range(2):
            own_ref[array, part] = source[part, slab]
    for distance, piece_ref in enumerate(piece_refs, 1):
        index = lax.rem(slab + distance, SLABS)
        head = jnp.zeros((16, Z), jnp.int32)
        for array, source in enumerate((initial_ref, measured_ref)):
            for part in range(2):
                block = 2 * array + part
                codes, power = encode(source[part, index])
                codes = codes.astype(jnp.int16)
                piece_ref[pl.ds(64 * block, 32), :] = codes[:, :Z]
                piece_ref[pl.ds(64 * block + 32, 32), :] = codes[:, Z:]
                head = jnp.where(row == block, power.astype(jnp.int32), head)
        piece_ref[pl.ds(256, 16), :] = head.astype(jnp.int16)


def arrange(slab, initial, measured, half):
    block = pl.BlockSpec((2, SLABS, 32, R), lambda i: (0, half, 0, 0))
    piece = jax.ShapeDtypeStruct((272, Z), jnp.int16)
    return pl.pallas_call(
        arrange_kernel,
        grid=(1,),
        out_shape=(jax.ShapeDtypeStruct((2, 2, 32, R), F32),) + (piece,) * 3,
        in_specs=[SMEM, block, block],
        out_specs=(VMEM,) * 4,
        compiler_params=pltpu.CompilerParams(vmem_limit_bytes=123 << 19),
        cost_estimate=cost(1 << 20, 1 << 20),
        name="arrange",
    )(slab, initial, measured)


def moved(values, offset, lane):
    source = lane + offset
    rolled = pltpu.roll(values, lax.rem(Z - offset, Z), 1)
    return jnp.where((source >= 0) & (source < Z), rolled, 0.0).astype(BF16)


def swap_blocks(blocks):
    lane = lax.broadcasted_iota(jnp.int32, blocks[0].shape, 1)
    odd32 = (lane // 32) % 2 == 1
    high64 = lane >= 64
    a, b, c, d = blocks
    for_pairs = []
    for low, high in ((a, b), (c, d)):
        for_pairs.append(
            (
                jnp.where(odd32, pltpu.roll(high, 32, 1), low),
                jnp.where(odd32, high, pltpu.roll(low, 96, 1)),
            )
        )
    (a, b), (c, d) = for_pairs
    out = [None] * 4
    for i, (low, high) in enumerate(((a, c), (b, d))):
        out[i] = jnp.where(high64, pltpu.roll(high, 64, 1), low)
        out[i + 2] = jnp.where(high64, high, pltpu.roll(low, 64, 1))
    return out


def passes(offsets_ref, projectors, iterates, measures, shifted):
    lane = lax.broadcasted_iota(jnp.int32, (R, Z), 1)

    def place(slot_sign, index, real, imag):
        for slot in range(3):
            rows = pl.ds(R * slot, R)
            offset = slot_sign * offsets_ref[slot]
            shifted[index, rows, :Z] = moved(real, offset, lane)
            shifted[index, rows, Z:] = moved(imag, offset, lane)

    def step(count, carry):
        for index, blocks in enumerate(projectors):
            iterate, measured = iterates[index], measures[index]
            place(1, index, iterate[0], iterate[1])
            by_real = dot(blocks[0], shifted[index])
            by_imag = dot(blocks[1], shifted[index])
            real = measured[0] - (by_real[:, :Z] - by_imag[:, Z:])
            imag = measured[1] - (by_imag[:, :Z] + by_real[:, Z:])
            place(-1, index, real.astype(BF16).astype(F32), imag.astype(BF16).astype(F32))
            by_real = dot(blocks[2], shifted[index])
            by_imag = dot(blocks[3], shifted[index])
            iterate[0] += STEP_SIZE * (by_real[:, :Z] + by_imag[:, Z:])
            iterate[1] += STEP_SIZE * (by_real[:, Z:] - by_imag[:, :Z])
        return carry

    lax.fori_loop(0, INNER, step, 0)


def pack(iterates, rows_ref, packed_ref):
    for half, iterate in enumerate(iterates):
        for part in range(2):
            blocks = [iterate[part, pl.ds(i, GROUPS, stride=4), :] for i in range(4)]
            for slab, block in enumerate(swap_blocks(blocks)):
                rows_ref[pl.ds(Q * slab + 2 * half + part, GROUPS, stride=4), :] = block
    packed_ref[...] = rows_ref[...].astype(packed_ref.dtype)


def load_blocks(blocks_far, blocks, sems, halves):
    copies = []
    for index, half in enumerate(halves):
        for kind in range(2):
            pair = pl.ds(2 * kind, 2)
            copy = pltpu.make_async_copy(
                blocks_far.at[half, pair], blocks.at[index, pair], sems.at[len(copies)]
            )
            copy.start()
            copies.append(copy)
    return copies


def gather(slab_ref, own, pieces, column, iterate, measured):
    slab = slab_ref[0]
    scales = [
        jnp.exp2(piece[pl.ds(256, 16), :].astype(jnp.int32).astype(F32)) * (1.0 / LEVELS)
        for piece in pieces
    ]
    for array, target in ((0, iterate), (1, measured)):
        for part in range(2):
            block = 2 * array + part
            column[pl.ds(pl.multiple_of(32 * slab, 32), 32), :] = own[array, part]
            for distance, (piece, scale) in enumerate(zip(pieces, scales), 1):
                rows = pl.ds(pl.multiple_of(32 * lax.rem(slab + 4 - distance, 4), 32), 32)
                for side in range(2):
                    codes = piece[pl.ds(64 * block + 32 * side, 32), :].astype(jnp.int32)
                    column[rows, Z * side : Z * (side + 1)] = codes.astype(F32) * scale[block : block + 1]
            target[part] = column[...].T


def early_kernel(
    slab_ref, offsets_ref, own, one, two, three, blocks_far,
    iterate, measured, column, shifted, blocks, sems,
):
    copies = load_blocks(blocks_far, blocks, sems, (0,))
    gather(slab_ref, own, (one, two, three), column, iterate, measured)
    for copy in copies:
        copy.wait()
    passes(offsets_ref, [blocks.at[0]], [iterate], [measured], shifted)


def late_kernel(
    slab_ref, offsets_ref, own, one, two, three, blocks_far, other,
    iterate, measured, packed_ref, column, shifted, blocks, sems, rows_ref,
):
    copies = load_blocks(blocks_far, blocks, sems, (1,))
    gather(slab_ref, own, (one, two, three), column, iterate, measured)
    for copy in copies:
        copy.wait()
    passes(offsets_ref, [blocks.at[0]], [iterate], [measured], shifted)
    pack([other, iterate], rows_ref, packed_ref)


def second_kernel(
    silent_ref, offsets_ref, packed_in, kept_0, kept_1, measured_0, measured_1, blocks_far,
    packed_ref, iterate, shifted, rows_ref, blocks, sems,
):
    copies = load_blocks(blocks_far, blocks, sems, (0, 1))
    rows_ref[...] = packed_in[...].astype(F32)
    silent = silent_ref[0] != 0
    for half, kept in enumerate((kept_0, kept_1)):
        for part in range(2):
            parts = [
                rows_ref[pl.ds(Q * slab + 2 * half + part, GROUPS, stride=4), :] for slab in range(4)
            ]
            for i, added in enumerate(swap_blocks(parts)):
                rows = pl.ds(i, GROUPS, stride=4)
                base = kept[part, rows, :]
                if half == 0 and part == 1:
                    base = jnp.where(silent, 0.0, base)
                iterate[half, part, rows, :] = base + added
    for copy in copies:
        copy.wait()
    iterates = [iterate.at[0], iterate.at[1]]
    passes(offsets_ref, [blocks.at[0], blocks.at[1]], iterates, [measured_0, measured_1], shifted)
    pack(iterates, rows_ref, packed_ref)


def pass_scratch(halves, sems):
    return [
        pltpu.VMEM((halves, 3 * R, 2 * Z), BF16),
        pltpu.VMEM((halves, 4, R, 3 * R), BF16),
        pltpu.SemaphoreType.DMA((sems,)),
    ]


ROWS = pltpu.VMEM((4 * Q, Z), F32)


def first_half(slab, offsets, pieces, blocks, other):
    late = other is not None
    return pl.pallas_call(
        late_kernel if late else early_kernel,
        out_shape=(SPECTRUM, SPECTRUM) + ((PACKED,) if late else ()),
        in_specs=[SMEM, SMEM] + [VMEM] * 4 + [HBM] + ([VMEM] if late else []),
        out_specs=(VMEM,) * (3 if late else 2),
        scratch_shapes=[pltpu.VMEM((Z, R), F32)] + pass_scratch(1, 2) + ([ROWS] if late else []),
        compiler_params=ALONE,
        cost_estimate=cost(1 << 30, 4 << 20),
        name="late" if late else "early",
    )(slab, offsets, *pieces, blocks, *((other,) if late else ()))


def later_half(silent, offsets, packed, kept, measures, blocks):
    shifted, held, sems = pass_scratch(2, 4)
    return pl.pallas_call(
        second_kernel,
        out_shape=PACKED,
        in_specs=[SMEM, SMEM] + [VMEM] * 5 + [HBM],
        out_specs=VMEM,
        scratch_shapes=[pltpu.VMEM((2, 2, R, Z), F32), shifted, ROWS, held, sems],
        compiler_params=ALONE,
        cost_estimate=cost(2 << 30, 8 << 20),
        name="later_half",
    )(silent, offsets, packed, *kept, *measures, blocks)


def to_volume(packed_ref, tables_ref, volume):
    def residue(c, rows):
        block = packed_ref[pl.ds(Q * c, Q), :]
        total = dot(tables_ref[0][rows, :], block)
        for table in tables_ref[1:]:
            total = total + dot(table[rows, :], block)
        return total

    zero = residue(0, pl.ds(0, Q))
    two = residue(2, pl.ds(Q, Q))
    same, other = zero + two, zero - two
    one = residue(1, pl.ds(2 * Q, 2 * Q))
    three = residue(3, pl.ds(4 * Q, 2 * Q))
    plain = one[:Q] + three[:Q]
    turned = one[Q:] - three[Q:]
    volume[pl.ds(8, Q), :] = same + plain
    volume[pl.ds(8 + Q, Q), :] = other + turned
    volume[pl.ds(8 + 2 * Q, Q), :] = same - plain
    volume[pl.ds(8 + 3 * Q, Q), :] = other - turned
    volume[7:8, :] = volume[A + 7 : A + 8, :]
    volume[A + 8 : A + 9, :] = volume[8:9, :]


def change(volume, start):
    here = volume[pl.ds(8 + start, Q), :]
    before = volume[pl.ds(7 + start, Q), :]
    after = volume[pl.ds(9 + start, Q), :]
    ahead = jnp.clip(after - here, -CLIP_LEVEL, CLIP_LEVEL)
    behind = jnp.clip(here - before, -CLIP_LEVEL, CLIP_LEVEL)
    return here, SMOOTHING * (ahead - behind)


def middle_kernel(packed_ref, angles_ref, even_ref, odd_ref, spectra_ref, volume):
    to_volume(packed_ref, [angles_ref], volume)
    quarters = [change(volume, Q * m)[1] for m in range(4)]
    same, cross = quarters[0] + quarters[2], quarters[1] + quarters[3]
    plain, turned = quarters[0] - quarters[2], quarters[1] - quarters[3]

    def put(c, table, *values):
        values = jnp.concatenate([v.astype(BF16) for v in values], axis=0)
        spectra_ref[pl.ds(Q * c, Q), :] = dot(table, values).astype(spectra_ref.dtype)

    put(0, even_ref[:Q], same + cross)
    put(2, even_ref[Q:], same - cross)
    put(1, odd_ref[:Q], plain, turned)
    put(3, odd_ref[Q:], plain, -turned)


def middle(packed, angles, even, odd):
    return pl.pallas_call(
        middle_kernel,
        out_shape=PACKED,
        in_specs=[VMEM] * 4,
        out_specs=VMEM,
        scratch_shapes=[pltpu.VMEM((A + 16, Z), F32)],
        compiler_params=PARAMS,
        cost_estimate=cost(1 << 30, 4 << 20),
        name="middle",
    )(packed, angles, even, odd)


def last_kernel(packed_ref, high_ref, low_ref, out_ref, volume):
    to_volume(packed_ref, [high_ref, low_ref], volume)
    for m in range(4):
        here, added = change(volume, Q * m)
        values = (here + added).T
        for i in range(4):
            out_ref[:, i, pl.ds(Q * m, Q)] = values[32 * i : 32 * (i + 1), :]


def last(packed, high, low):
    return pl.pallas_call(
        last_kernel,
        out_shape=jax.ShapeDtypeStruct((Z // SLABS, R // GROUPS, A), F32),
        in_specs=[VMEM] * 3,
        out_specs=VMEM,
        scratch_shapes=[pltpu.VMEM((A + 16, Z), F32)],
        compiler_params=PARAMS,
        cost_estimate=cost(1 << 29, 4 << 20),
        name="last",
    )(packed, high, low)


def exchange(packed):
    blocks = packed.reshape(SLABS * GROUPS, 4, Z)
    return lax.all_to_all(blocks, ("slab", "freq"), 0, 0, tiled=True).reshape(packed.shape)


def spread(slab, initial, measured, half):
    own, *pieces = arrange(slab, initial, measured, half)
    for distance, piece in enumerate(pieces, 1):
        pairs = [(i, (i + distance) % SLABS) for i in range(SLABS)]
        pieces[distance - 1] = lax.ppermute(piece, "slab", pairs)
    return [own, *pieces]


def on_device(initial, measured, projector, offsets):
    (angles, angles_low), (even, _), (odd, _) = tables()
    slab = lax.axis_index("slab").astype(jnp.int32)
    group = lax.axis_index("freq").astype(jnp.int32)
    silent = ((slab == 0) & (group == 0)).astype(jnp.int32).reshape(1)
    slab = slab.reshape(1)
    pieces = [spread(slab, initial, measured, half) for half in range(2)]
    blocks = prepare(slab, projector)
    kept_0, measured_0 = first_half(slab, offsets, pieces[0], blocks, None)
    late, kept_0 = lax.optimization_barrier((pieces[1], kept_0))
    kept_1, measured_1, packed = first_half(slab, offsets, late, blocks, kept_0)
    packed = exchange(middle(exchange(packed), angles, even, odd))
    packed = later_half(silent, offsets, packed, (kept_0, kept_1), (measured_0, measured_1), blocks)
    return last(exchange(packed), angles, angles_low)


def solution(mesh):
    placed = (
        P(None, "freq", "slab", None),
        P(None, "freq", "slab", None),
        P(None, None, "freq", None, None),
        P(),
    )
    return jax.shard_map(
        on_device, mesh=mesh, in_specs=placed, out_specs=P("slab", "freq", None), check_vma=False
    )
```

```python
import math

import jax
import jax.numpy as jnp
import numpy as np
from jax import lax
from jax.experimental import pallas as pl
from jax.experimental.pallas import tpu as pltpu
from jax.sharding import PartitionSpec as P

A = 1024
Q = A // 4
STEP_SIZE = 0.25
CLIP_LEVEL = 1.0
SMOOTHING = 0.25
INNER = 2
SLABS = 4
GROUPS = 64
Z = 128
R = 256
F32 = jnp.float32
BF16 = jnp.bfloat16
LEVELS = 32000.0
VMEM = pl.BlockSpec(memory_space=pltpu.VMEM)
SMEM = pl.BlockSpec(memory_space=pltpu.SMEM)
HBM = pl.BlockSpec(memory_space=pltpu.HBM)


def split_table(table):
    high = table.astype(np.float32).astype(jnp.bfloat16)
    low = (table - high.astype(np.float64)).astype(np.float32).astype(jnp.bfloat16)
    return high, low


def tables():
    group, half, part = np.meshgrid(np.arange(GROUPS), np.arange(2), np.arange(2), indexing="ij")
    plain, turned, weights = [], [], []
    for residue in range(4):
        k = (8 * group + residue + 4 * half).reshape(-1)
        imag = part.reshape(-1)[:, None] == 1
        phase = (k[:, None] * np.arange(Q)[None, :] % A) * (2.0 * math.pi / A)
        plain.append(np.where(imag, -np.sin(phase), np.cos(phase)) / math.sqrt(A))
        turned.append(np.where(imag, -np.cos(phase), -np.sin(phase)) / math.sqrt(A))
        weights.append(np.where(k == 0, 1.0, 2.0)[:, None])
    synth = [(p * w).T for p, w in zip(plain, weights)]
    synth_turned = [(t * w).T for t, w in zip(turned, weights)]
    to_angles = np.concatenate(
        [synth[0], synth[2], synth[1], synth_turned[1], synth[3], synth_turned[3]], axis=0
    )
    even = np.concatenate([plain[0], plain[2]], axis=0)
    odd = np.concatenate(
        [np.concatenate([plain[c], turned[c]], axis=1) for c in (1, 3)], axis=0
    )
    return split_table(to_angles), split_table(even), split_table(odd)


def cost(flops, size):
    return pl.CostEstimate(flops=flops, bytes_accessed=size, transcendentals=0)


PARAMS = pltpu.CompilerParams(vmem_limit_bytes=20 << 20)
ALONE = pltpu.CompilerParams(vmem_limit_bytes=100 << 19)
SPECTRUM = jax.ShapeDtypeStruct((2, 2, R, Z), F32)
PACKED = jax.ShapeDtypeStruct((4 * Q, Z), BF16)


def dot(left, right):
    return jnp.dot(left, right, preferred_element_type=F32)


def prepare_kernel(slab_ref, projector_ref, blocks_ref, blocks, sems):
    slab = slab_ref[0]
    loads, stores = [], []
    for half in range(2):
        for part in range(2):
            for slot in range(3):
                copy = pltpu.make_async_copy(
                    projector_ref.at[slot, part, slab + 4 * half],
                    blocks.at[half, 2 + part, :, pl.ds(R * slot, R)],
                    sems.at[len(loads)],
                )
                copy.start()
                loads.append(copy)
    for half in range(2):
        for part in range(2):
            for slot in range(3):
                loads[6 * half + 3 * part + slot].wait()
                cols = pl.ds(R * slot, R)
                blocks[half, part, :, cols] = blocks[half, 2 + part, :, cols].T
        copy = pltpu.make_async_copy(blocks.at[half], blocks_ref.at[half], sems.at[12 + half])
        copy.start()
        stores.append(copy)
    for copy in stores:
        copy.wait()


def prepare(slab, projector):
    return pl.pallas_call(
        prepare_kernel,
        out_shape=jax.ShapeDtypeStruct((4, 4, R, 3 * R), BF16),
        in_specs=[SMEM, HBM],
        out_specs=HBM,
        scratch_shapes=[pltpu.VMEM((2, 4, R, 3 * R), BF16), pltpu.SemaphoreType.DMA((14,))],
        compiler_params=ALONE,
        cost_estimate=cost(0, 8 << 20),
        name="prepare",
    )(slab, projector)


def encode(values):
    largest = jnp.max(jnp.max(jnp.abs(values), axis=1, keepdims=True), axis=0, keepdims=True)
    power = jnp.clip(jnp.ceil(jnp.log2(largest)), -100.0, 100.0)
    return jnp.round(values * (LEVELS * jnp.exp2(-power))).astype(jnp.int32), power


def arrange_kernel(initial_ref, measured_ref, piece_ref):
    row = lax.broadcasted_iota(jnp.int32, (16, Z), 0)
    head = jnp.zeros((16, Z), jnp.int32)
    for array, source in enumerate((initial_ref, measured_ref)):
        for part in range(2):
            for half in range(2):
                block = 4 * half + 2 * array + part
                codes, power = encode(source[part, half, 0])
                codes = codes.astype(jnp.int16)
                piece_ref[0, pl.ds(64 * block, 32), :] = codes[:, :Z]
                piece_ref[0, pl.ds(64 * block + 32, 32), :] = codes[:, Z:]
                head = jnp.where(row == block, power.astype(jnp.int32), head)
    piece_ref[0, pl.ds(512, 16), :] = head.astype(jnp.int16)


def arrange(initial, measured):
    shape = (2, 2, SLABS, 32, R)
    block = pl.BlockSpec((2, 2, 1, 32, R), lambda d: (0, 0, d, 0, 0))
    return pl.pallas_call(
        arrange_kernel,
        grid=(SLABS,),
        out_shape=jax.ShapeDtypeStruct((SLABS, 528, Z), jnp.int16),
        in_specs=[block, block],
        out_specs=pl.BlockSpec((1, 528, Z), lambda d: (d, 0, 0)),
        compiler_params=pltpu.CompilerParams(vmem_limit_bytes=123 << 19),
        cost_estimate=cost(1 << 20, 1 << 20),
        name="arrange",
    )(initial.reshape(shape), measured.reshape(shape))


def moved(values, offset, lane):
    source = lane + offset
    rolled = pltpu.roll(values, lax.rem(Z - offset, Z), 1)
    return jnp.where((source >= 0) & (source < Z), rolled, 0.0).astype(BF16)


def swap_blocks(blocks):
    lane = lax.broadcasted_iota(jnp.int32, blocks[0].shape, 1)
    odd32 = (lane // 32) % 2 == 1
    high64 = lane >= 64
    a, b, c, d = blocks
    for_pairs = []
    for low, high in ((a, b), (c, d)):
        for_pairs.append(
            (
                jnp.where(odd32, pltpu.roll(high, 32, 1), low),
                jnp.where(odd32, high, pltpu.roll(low, 96, 1)),
            )
        )
    (a, b), (c, d) = for_pairs
    out = [None] * 4
    for i, (low, high) in enumerate(((a, c), (b, d))):
        out[i] = jnp.where(high64, pltpu.roll(high, 64, 1), low)
        out[i + 2] = jnp.where(high64, high, pltpu.roll(low, 64, 1))
    return out


def passes(offsets_ref, projectors, iterates, measures, shifted):
    lane = lax.broadcasted_iota(jnp.int32, (R, Z), 1)

    def place(slot_sign, index, real, imag):
        for slot in range(3):
            rows = pl.ds(R * slot, R)
            offset = slot_sign * offsets_ref[slot]
            shifted[index, rows, :Z] = moved(real, offset, lane)
            shifted[index, rows, Z:] = moved(imag, offset, lane)

    def product(kind, index):
        by_real = dot(projectors[index][kind], shifted[index])
        by_imag = dot(projectors[index][kind + 1], shifted[index])
        return by_real, by_imag

    both = range(len(projectors))

    def step(count, carry):
        for index in both:
            place(1, index, iterates[index][0], iterates[index][1])
        products = [product(0, index) for index in both]
        for index, (by_real, by_imag) in zip(both, products):
            real = measures[index][0] - (by_real[:, :Z] - by_imag[:, Z:])
            imag = measures[index][1] - (by_imag[:, :Z] + by_real[:, Z:])
            place(-1, index, real.astype(BF16).astype(F32), imag.astype(BF16).astype(F32))
        products = [product(2, index) for index in both]
        for index, (by_real, by_imag) in zip(both, products):
            iterates[index][0] += STEP_SIZE * (by_real[:, :Z] + by_imag[:, Z:])
            iterates[index][1] += STEP_SIZE * (by_real[:, Z:] - by_imag[:, :Z])
        return carry

    lax.fori_loop(0, INNER, step, 0)


def pack(iterates, rows_ref, packed_ref):
    for half, iterate in enumerate(iterates):
        for part in range(2):
            blocks = [iterate[part, pl.ds(i, GROUPS, stride=4), :] for i in range(4)]
            for slab, block in enumerate(swap_blocks(blocks)):
                rows_ref[pl.ds(Q * slab + 2 * half + part, GROUPS, stride=4), :] = block
    packed_ref[...] = rows_ref[...].astype(packed_ref.dtype)


def load_blocks(blocks_far, blocks, sems, halves):
    copies = []
    for index, half in enumerate(halves):
        for kind in range(2):
            pair = pl.ds(2 * kind, 2)
            copy = pltpu.make_async_copy(
                blocks_far.at[half, pair], blocks.at[index, pair], sems.at[len(copies)]
            )
            copy.start()
            copies.append(copy)
    return copies


def gather(pieces, column, iterate, measured):
    for slab in range(SLABS):
        power = pieces[slab, pl.ds(512, 16), :].astype(jnp.int32).astype(F32)
        scale = jnp.exp2(power) * (1.0 / LEVELS)
        for block in range(8):
            for side in range(2):
                codes = pieces[slab, pl.ds(64 * block + 32 * side, 32), :].astype(jnp.int32)
                rows = pl.ds(32 * slab, 32)
                column[block, rows, Z * side : Z * (side + 1)] = codes.astype(F32) * scale[block : block + 1]
    for half in range(2):
        for part in range(2):
            iterate[half, part] = column[4 * half + part].T
            measured[half, part] = column[4 * half + 2 + part].T


def first_kernel(
    offsets_ref, pieces, blocks_far,
    iterate, measured, packed_ref, column, rows_ref, shifted, blocks, sems,
):
    copies = load_blocks(blocks_far, blocks, sems, (0, 1))
    gather(pieces, column, iterate, measured)
    for copy in copies:
        copy.wait()
    halves = range(2)
    iterates = [iterate.at[half] for half in halves]
    passes(offsets_ref, [blocks.at[h] for h in halves], iterates, [measured.at[h] for h in halves], shifted)
    pack(iterates, rows_ref, packed_ref)


def second_kernel(
    silent_ref, offsets_ref, packed_in, kept, measured, blocks_far,
    packed_ref, iterate, rows_ref, shifted, blocks, sems,
):
    copies = load_blocks(blocks_far, blocks, sems, (0, 1))
    rows_ref[...] = packed_in[...].astype(F32)
    silent = silent_ref[0] != 0
    for half in range(2):
        for part in range(2):
            parts = [
                rows_ref[pl.ds(Q * slab + 2 * half + part, GROUPS, stride=4), :] for slab in range(4)
            ]
            for i, added in enumerate(swap_blocks(parts)):
                rows = pl.ds(i, GROUPS, stride=4)
                base = kept[half, part, rows, :]
                if half == 0 and part == 1:
                    base = jnp.where(silent, 0.0, base)
                iterate[half, part, rows, :] = base + added
    for copy in copies:
        copy.wait()
    iterates = [iterate.at[0], iterate.at[1]]
    measures = [measured.at[0], measured.at[1]]
    passes(offsets_ref, [blocks.at[0], blocks.at[1]], iterates, measures, shifted)
    pack(iterates, rows_ref, packed_ref)


PASS_SCRATCH = [
    pltpu.VMEM((4 * Q, Z), F32),
    pltpu.VMEM((2, 3 * R, 2 * Z), BF16),
    pltpu.VMEM((2, 4, R, 3 * R), BF16),
    pltpu.SemaphoreType.DMA((4,)),
]


def first_half(offsets, pieces, blocks):
    return pl.pallas_call(
        first_kernel,
        out_shape=(SPECTRUM, SPECTRUM, PACKED),
        in_specs=[SMEM, VMEM, HBM],
        out_specs=(VMEM,) * 3,
        scratch_shapes=[pltpu.VMEM((8, Z, R), F32)] + PASS_SCRATCH,
        compiler_params=ALONE,
        cost_estimate=cost(2 << 30, 8 << 20),
        name="first_half",
    )(offsets, pieces, blocks)


def later_half(silent, offsets, packed, kept, measured, blocks):
    return pl.pallas_call(
        second_kernel,
        out_shape=PACKED,
        in_specs=[SMEM, SMEM] + [VMEM] * 3 + [HBM],
        out_specs=VMEM,
        scratch_shapes=[pltpu.VMEM((2, 2, R, Z), F32)] + PASS_SCRATCH,
        compiler_params=ALONE,
        cost_estimate=cost(2 << 30, 8 << 20),
        name="later_half",
    )(silent, offsets, packed, kept, measured, blocks)


def to_volume(packed_ref, tables_ref, volume):
    def residue(c, rows):
        block = packed_ref[pl.ds(Q * c, Q), :]
        total = dot(tables_ref[0][rows, :], block)
        for table in tables_ref[1:]:
            total = total + dot(table[rows, :], block)
        return total

    zero = residue(0, pl.ds(0, Q))
    two = residue(2, pl.ds(Q, Q))
    same, other = zero + two, zero - two
    one = residue(1, pl.ds(2 * Q, 2 * Q))
    three = residue(3, pl.ds(4 * Q, 2 * Q))
    plain = one[:Q] + three[:Q]
    turned = one[Q:] - three[Q:]
    volume[pl.ds(8, Q), :] = same + plain
    volume[pl.ds(8 + Q, Q), :] = other + turned
    volume[pl.ds(8 + 2 * Q, Q), :] = same - plain
    volume[pl.ds(8 + 3 * Q, Q), :] = other - turned
    volume[7:8, :] = volume[A + 7 : A + 8, :]
    volume[A + 8 : A + 9, :] = volume[8:9, :]


def change(volume, start):
    here = volume[pl.ds(8 + start, Q), :]
    before = volume[pl.ds(7 + start, Q), :]
    after = volume[pl.ds(9 + start, Q), :]
    ahead = jnp.clip(after - here, -CLIP_LEVEL, CLIP_LEVEL)
    behind = jnp.clip(here - before, -CLIP_LEVEL, CLIP_LEVEL)
    return here, SMOOTHING * (ahead - behind)


def middle_kernel(packed_ref, angles_ref, even_ref, odd_ref, spectra_ref, volume):
    to_volume(packed_ref, [angles_ref], volume)
    quarters = [change(volume, Q * m)[1] for m in range(4)]
    same, cross = quarters[0] + quarters[2], quarters[1] + quarters[3]
    plain, turned = quarters[0] - quarters[2], quarters[1] - quarters[3]

    def put(c, table, *values):
        values = jnp.concatenate([v.astype(BF16) for v in values], axis=0)
        spectra_ref[pl.ds(Q * c, Q), :] = dot(table, values).astype(spectra_ref.dtype)

    put(0, even_ref[:Q], same + cross)
    put(2, even_ref[Q:], same - cross)
    put(1, odd_ref[:Q], plain, turned)
    put(3, odd_ref[Q:], plain, -turned)


def middle(packed, angles, even, odd):
    return pl.pallas_call(
        middle_kernel,
        out_shape=PACKED,
        in_specs=[VMEM] * 4,
        out_specs=VMEM,
        scratch_shapes=[pltpu.VMEM((A + 16, Z), F32)],
        compiler_params=PARAMS,
        cost_estimate=cost(1 << 30, 4 << 20),
        name="middle",
    )(packed, angles, even, odd)


def last_kernel(packed_ref, high_ref, low_ref, out_ref, volume):
    to_volume(packed_ref, [high_ref, low_ref], volume)
    for m in range(4):
        here, added = change(volume, Q * m)
        values = (here + added).T
        for i in range(4):
            out_ref[:, i, pl.ds(Q * m, Q)] = values[32 * i : 32 * (i + 1), :]


def last(packed, high, low):
    return pl.pallas_call(
        last_kernel,
        out_shape=jax.ShapeDtypeStruct((Z // SLABS, R // GROUPS, A), F32),
        in_specs=[VMEM] * 3,
        out_specs=VMEM,
        scratch_shapes=[pltpu.VMEM((A + 16, Z), F32)],
        compiler_params=PARAMS,
        cost_estimate=cost(1 << 29, 4 << 20),
        name="last",
    )(packed, high, low)


def exchange(packed):
    blocks = packed.reshape(SLABS * GROUPS, 4, Z)
    return lax.all_to_all(blocks, ("slab", "freq"), 0, 0, tiled=True).reshape(packed.shape)


def on_device(initial, measured, projector, offsets):
    (angles, angles_low), (even, _), (odd, _) = tables()
    slab = lax.axis_index("slab").astype(jnp.int32)
    group = lax.axis_index("freq").astype(jnp.int32)
    silent = ((slab == 0) & (group == 0)).astype(jnp.int32).reshape(1)
    pieces = lax.all_to_all(arrange(initial, measured), "slab", 0, 0, tiled=True)
    blocks = prepare(slab.reshape(1), projector)
    kept, measured, packed = first_half(offsets, pieces, blocks)
    packed = exchange(middle(exchange(packed), angles, even, odd))
    packed = later_half(silent, offsets, packed, kept, measured, blocks)
    return last(exchange(packed), angles, angles_low)


def solution(mesh):
    placed = (
        P(None, "freq", "slab", None),
        P(None, "freq", "slab", None),
        P(None, None, "freq", None, None),
        P(),
    )
    return jax.shard_map(
        on_device, mesh=mesh, in_specs=placed, out_specs=P("slab", "freq", None), check_vma=False
    )
```

```python
import math

import jax
import jax.numpy as jnp
import numpy as np
from jax import lax
from jax.experimental import pallas as pl
from jax.experimental.pallas import tpu as pltpu
from jax.sharding import PartitionSpec as P

A = 1024
Q = A // 4
STEP_SIZE = 0.25
CLIP_LEVEL = 1.0
SMOOTHING = 0.25
INNER = 2
SLABS = 4
GROUPS = 64
Z = 128
R = 256
F32 = jnp.float32
BF16 = jnp.bfloat16
LEVELS = 32000.0
VMEM = pl.BlockSpec(memory_space=pltpu.VMEM)
SMEM = pl.BlockSpec(memory_space=pltpu.SMEM)
HBM = pl.BlockSpec(memory_space=pltpu.HBM)


def split_table(table):
    high = table.astype(np.float32).astype(jnp.bfloat16)
    low = (table - high.astype(np.float64)).astype(np.float32).astype(jnp.bfloat16)
    return high, low


def tables():
    group, half, part = np.meshgrid(np.arange(GROUPS), np.arange(2), np.arange(2), indexing="ij")
    plain, turned, weights = [], [], []
    for residue in range(4):
        k = (8 * group + residue + 4 * half).reshape(-1)
        imag = part.reshape(-1)[:, None] == 1
        phase = (k[:, None] * np.arange(Q)[None, :] % A) * (2.0 * math.pi / A)
        plain.append(np.where(imag, -np.sin(phase), np.cos(phase)) / math.sqrt(A))
        turned.append(np.where(imag, -np.cos(phase), -np.sin(phase)) / math.sqrt(A))
        weights.append(np.where(k == 0, 1.0, 2.0)[:, None])
    synth = [(p * w).T for p, w in zip(plain, weights)]
    synth_turned = [(t * w).T for t, w in zip(turned, weights)]
    to_angles = np.concatenate(
        [synth[0], synth[2], synth[1], synth_turned[1], synth[3], synth_turned[3]], axis=0
    )
    even = np.concatenate([plain[0], plain[2]], axis=0)
    odd = np.concatenate(
        [np.concatenate([plain[c], turned[c]], axis=1) for c in (1, 3)], axis=0
    )
    return split_table(to_angles), split_table(even), split_table(odd)


def cost(flops, size):
    return pl.CostEstimate(flops=flops, bytes_accessed=size, transcendentals=0)


PARAMS = pltpu.CompilerParams(vmem_limit_bytes=20 << 20)
ALONE = pltpu.CompilerParams(vmem_limit_bytes=100 << 19)
SPECTRUM = jax.ShapeDtypeStruct((2, 2, R, Z), F32)
PACKED = jax.ShapeDtypeStruct((4 * Q, Z), BF16)


def dot(left, right):
    return jnp.dot(left, right, preferred_element_type=F32)


def prepare_kernel(slab_ref, projector_ref, blocks_ref, blocks, sems):
    slab = slab_ref[0]
    loads, stores = [], []
    for half in range(2):
        for part in range(2):
            for slot in range(3):
                copy = pltpu.make_async_copy(
                    projector_ref.at[slot, part, slab + 4 * half],
                    blocks.at[half, 2 + part, :, pl.ds(R * slot, R)],
                    sems.at[len(loads)],
                )
                copy.start()
                loads.append(copy)
    for half in range(2):
        for part in range(2):
            for slot in range(3):
                loads[6 * half + 3 * part + slot].wait()
                cols = pl.ds(R * slot, R)
                blocks[half, part, :, cols] = blocks[half, 2 + part, :, cols].T
        copy = pltpu.make_async_copy(blocks.at[half], blocks_ref.at[half], sems.at[12 + half])
        copy.start()
        stores.append(copy)
    for copy in stores:
        copy.wait()


def prepare(slab, projector):
    return pl.pallas_call(
        prepare_kernel,
        out_shape=jax.ShapeDtypeStruct((4, 4, R, 3 * R), BF16),
        in_specs=[SMEM, HBM],
        out_specs=HBM,
        scratch_shapes=[pltpu.VMEM((2, 4, R, 3 * R), BF16), pltpu.SemaphoreType.DMA((14,))],
        compiler_params=ALONE,
        cost_estimate=cost(0, 8 << 20),
        name="prepare",
    )(slab, projector)


def encode(values):
    largest = jnp.max(jnp.max(jnp.abs(values), axis=1, keepdims=True), axis=0, keepdims=True)
    power = jnp.clip(jnp.ceil(jnp.log2(largest)), -100.0, 100.0)
    return jnp.round(values * (LEVELS * jnp.exp2(-power))).astype(jnp.int32), power


def arrange_kernel(initial_ref, measured_ref, pieces_ref, source, pieces, sems):
    loads, stores = [], []
    for chunk in range(4):
        far = (initial_ref, measured_ref)[chunk // 2].at[chunk % 2]
        loads.append(pltpu.make_async_copy(far, source.at[chunk], sems.at[chunk]))
        loads[-1].start()
    row = lax.broadcasted_iota(jnp.int32, (16, Z), 0)
    heads = [jnp.zeros((16, Z), jnp.int32)] * SLABS
    for chunk in range(4):
        loads[chunk].wait()
        for slab in range(SLABS):
            for half in range(2):
                block = 2 * chunk + half
                codes, power = encode(source[chunk, slab + 4 * half])
                codes = codes.astype(jnp.int16)
                pieces[slab, pl.ds(64 * block, 32), :] = codes[:, :Z]
                pieces[slab, pl.ds(64 * block + 32, 32), :] = codes[:, Z:]
                heads[slab] = jnp.where(row == block, power.astype(jnp.int32), heads[slab])
        rows = pl.ds(128 * chunk, 128)
        if chunk == 3:
            for slab in range(SLABS):
                pieces[slab, pl.ds(512, 16), :] = heads[slab].astype(jnp.int16)
            rows = pl.ds(384, 144)
        stores.append(
            pltpu.make_async_copy(pieces.at[:, rows], pieces_ref.at[:, rows], sems.at[4 + chunk])
        )
        stores[-1].start()
    for copy in stores:
        copy.wait()


def arrange(initial, measured):
    return pl.pallas_call(
        arrange_kernel,
        out_shape=jax.ShapeDtypeStruct((SLABS, 528, Z), jnp.int16),
        in_specs=[HBM, HBM],
        out_specs=HBM,
        scratch_shapes=[
            pltpu.VMEM((4, 2 * SLABS, 32, R), F32),
            pltpu.VMEM((SLABS, 528, Z), jnp.int16),
            pltpu.SemaphoreType.DMA((8,)),
        ],
        compiler_params=pltpu.CompilerParams(vmem_limit_bytes=126 << 19),
        cost_estimate=cost(1 << 20, 1 << 20),
        name="arrange",
    )(initial, measured)


def moved(values, offset, lane):
    source = lane + offset
    rolled = pltpu.roll(values, lax.rem(Z - offset, Z), 1)
    return jnp.where((source >= 0) & (source < Z), rolled, 0.0).astype(BF16)


def swap_blocks(blocks):
    lane = lax.broadcasted_iota(jnp.int32, blocks[0].shape, 1)
    odd32 = (lane // 32) % 2 == 1
    high64 = lane >= 64
    a, b, c, d = blocks
    for_pairs = []
    for low, high in ((a, b), (c, d)):
        for_pairs.append(
            (
                jnp.where(odd32, pltpu.roll(high, 32, 1), low),
                jnp.where(odd32, high, pltpu.roll(low, 96, 1)),
            )
        )
    (a, b), (c, d) = for_pairs
    out = [None] * 4
    for i, (low, high) in enumerate(((a, c), (b, d))):
        out[i] = jnp.where(high64, pltpu.roll(high, 64, 1), low)
        out[i + 2] = jnp.where(high64, high, pltpu.roll(low, 64, 1))
    return out


def passes(offsets_ref, blocks_far, iterate, measured, buffers, begin):
    packed_ref, rows_ref, shifted, blocks, sems = buffers
    lane = lax.broadcasted_iota(jnp.int32, (R, Z), 1)
    loads = [
        pltpu.make_async_copy(blocks_far.at[half], blocks.at[half], sems.at[half]) for half in range(2)
    ]
    for copy in loads:
        copy.start()

    def place(sign, half, real, imag):
        for slot in range(3):
            rows = pl.ds(R * slot, R)
            offset = sign * offsets_ref[slot]
            shifted[half, rows, :Z] = moved(real, offset, lane)
            shifted[half, rows, Z:] = moved(imag, offset, lane)

    def place_iterate(half):
        place(1, half, iterate[half, 0], iterate[half, 1])

    def product(kind, half):
        by_real = dot(blocks[half, kind], shifted[half])
        by_imag = dot(blocks[half, kind + 1], shifted[half])
        return by_real, by_imag

    def place_residual(half, by_real, by_imag):
        real = measured[half, 0] - (by_real[:, :Z] - by_imag[:, Z:])
        imag = measured[half, 1] - (by_imag[:, :Z] + by_real[:, Z:])
        place(-1, half, real.astype(BF16).astype(F32), imag.astype(BF16).astype(F32))

    def update(half, by_real, by_imag):
        iterate[half, 0] += STEP_SIZE * (by_real[:, :Z] + by_imag[:, Z:])
        iterate[half, 1] += STEP_SIZE * (by_real[:, Z:] - by_imag[:, :Z])

    begin(0)
    begin(1)
    loads[0].wait()
    place_iterate(0)
    place_iterate(1)
    first = product(0, 0)
    loads[1].wait()
    second = product(0, 1)
    for count in range(INNER):
        if count:
            first = product(0, 0)
            second = product(0, 1)
        place_residual(0, *first)
        place_residual(1, *second)
        first = product(2, 0)
        second = product(2, 1)
        update(0, *first)
        update(1, *second)
        if count + 1 < INNER:
            place_iterate(0)
            place_iterate(1)
    pack(0, iterate, rows_ref)
    pack(1, iterate, rows_ref)
    packed_ref[...] = rows_ref[...].astype(packed_ref.dtype)


def pack(half, iterate, rows_ref):
    for part in range(2):
        blocks = [iterate[half, part, pl.ds(i, GROUPS, stride=4), :] for i in range(4)]
        for slab, block in enumerate(swap_blocks(blocks)):
            rows_ref[pl.ds(Q * slab + 2 * half + part, GROUPS, stride=4), :] = block


def first_kernel(offsets_ref, pieces, blocks_far, iterate, measured, packed_ref, column, *scratch):
    scales = []
    for slab in range(SLABS):
        power = pieces[slab, pl.ds(512, 16), :].astype(jnp.int32).astype(F32)
        scales.append(jnp.exp2(power) * (1.0 / LEVELS))

    def begin(half):
        for chunk in range(4):
            block = 2 * chunk + half
            for slab in range(SLABS):
                for side in range(2):
                    codes = pieces[slab, pl.ds(64 * block + 32 * side, 32), :].astype(jnp.int32)
                    values = codes.astype(F32) * scales[slab][block : block + 1]
                    column[block, pl.ds(32 * slab, 32), Z * side : Z * (side + 1)] = values
            (iterate, measured)[chunk // 2][half, chunk % 2] = column[block].T

    passes(offsets_ref, blocks_far, iterate, measured, (packed_ref, *scratch), begin)


def second_kernel(
    silent_ref, offsets_ref, packed_in, kept, measured, blocks_far,
    packed_ref, arrived, iterate, *scratch,
):
    silent = silent_ref[0] != 0
    arrived[...] = packed_in[...].astype(F32)

    def begin(half):
        for part in range(2):
            parts = [
                arrived[pl.ds(Q * slab + 2 * half + part, GROUPS, stride=4), :] for slab in range(4)
            ]
            for i, added in enumerate(swap_blocks(parts)):
                rows = pl.ds(i, GROUPS, stride=4)
                base = kept[half, part, rows, :]
                if half == 0 and part == 1:
                    base = jnp.where(silent, 0.0, base)
                iterate[half, part, rows, :] = base + added

    passes(offsets_ref, blocks_far, iterate, measured, (packed_ref, *scratch), begin)


PASS_SCRATCH = [
    pltpu.VMEM((4 * Q, Z), F32),
    pltpu.VMEM((2, 3 * R, 2 * Z), BF16),
    pltpu.VMEM((2, 4, R, 3 * R), BF16),
    pltpu.SemaphoreType.DMA((2,)),
]


def first_half(offsets, pieces, blocks):
    return pl.pallas_call(
        first_kernel,
        out_shape=(SPECTRUM, SPECTRUM, PACKED),
        in_specs=[SMEM, VMEM, HBM],
        out_specs=(VMEM,) * 3,
        scratch_shapes=[pltpu.VMEM((8, Z, R), F32)] + PASS_SCRATCH,
        compiler_params=ALONE,
        cost_estimate=cost(2 << 30, 8 << 20),
        name="first_half",
    )(offsets, pieces, blocks)


def later_half(silent, offsets, packed, kept, measured, blocks):
    return pl.pallas_call(
        second_kernel,
        out_shape=PACKED,
        in_specs=[SMEM, SMEM] + [VMEM] * 3 + [HBM],
        out_specs=VMEM,
        scratch_shapes=[pltpu.VMEM((4 * Q, Z), F32), pltpu.VMEM((2, 2, R, Z), F32)] + PASS_SCRATCH,
        compiler_params=ALONE,
        cost_estimate=cost(2 << 30, 8 << 20),
        name="later_half",
    )(silent, offsets, packed, kept, measured, blocks)


def to_volume(packed_ref, tables_ref, volume):
    def residue(c, rows):
        block = packed_ref[pl.ds(Q * c, Q), :]
        total = dot(tables_ref[0][rows, :], block)
        for table in tables_ref[1:]:
            total = total + dot(table[rows, :], block)
        return total

    zero = residue(0, pl.ds(0, Q))
    two = residue(2, pl.ds(Q, Q))
    same, other = zero + two, zero - two
    one = residue(1, pl.ds(2 * Q, 2 * Q))
    three = residue(3, pl.ds(4 * Q, 2 * Q))
    plain = one[:Q] + three[:Q]
    turned = one[Q:] - three[Q:]
    volume[pl.ds(8, Q), :] = same + plain
    volume[pl.ds(8 + Q, Q), :] = other + turned
    volume[pl.ds(8 + 2 * Q, Q), :] = same - plain
    volume[pl.ds(8 + 3 * Q, Q), :] = other - turned
    volume[7:8, :] = volume[A + 7 : A + 8, :]
    volume[A + 8 : A + 9, :] = volume[8:9, :]


def change(volume, start):
    here = volume[pl.ds(8 + start, Q), :]
    before = volume[pl.ds(7 + start, Q), :]
    after = volume[pl.ds(9 + start, Q), :]
    ahead = jnp.clip(after - here, -CLIP_LEVEL, CLIP_LEVEL)
    behind = jnp.clip(here - before, -CLIP_LEVEL, CLIP_LEVEL)
    return here, SMOOTHING * (ahead - behind)


def middle_kernel(packed_ref, angles_ref, even_ref, odd_ref, spectra_ref, volume):
    to_volume(packed_ref, [angles_ref], volume)
    quarters = [change(volume, Q * m)[1] for m in range(4)]
    same, cross = quarters[0] + quarters[2], quarters[1] + quarters[3]
    plain, turned = quarters[0] - quarters[2], quarters[1] - quarters[3]

    def put(c, table, *values):
        values = jnp.concatenate([v.astype(BF16) for v in values], axis=0)
        spectra_ref[pl.ds(Q * c, Q), :] = dot(table, values).astype(spectra_ref.dtype)

    put(0, even_ref[:Q], same + cross)
    put(2, even_ref[Q:], same - cross)
    put(1, odd_ref[:Q], plain, turned)
    put(3, odd_ref[Q:], plain, -turned)


def middle(packed, angles, even, odd):
    return pl.pallas_call(
        middle_kernel,
        out_shape=PACKED,
        in_specs=[VMEM] * 4,
        out_specs=VMEM,
        scratch_shapes=[pltpu.VMEM((A + 16, Z), F32)],
        compiler_params=PARAMS,
        cost_estimate=cost(1 << 30, 4 << 20),
        name="middle",
    )(packed, angles, even, odd)


def last_kernel(packed_ref, high_ref, low_ref, out_ref, volume):
    to_volume(packed_ref, [high_ref, low_ref], volume)
    for m in range(4):
        here, added = change(volume, Q * m)
        values = (here + added).T
        for i in range(4):
            out_ref[:, i, pl.ds(Q * m, Q)] = values[32 * i : 32 * (i + 1), :]


def last(packed, high, low):
    return pl.pallas_call(
        last_kernel,
        out_shape=jax.ShapeDtypeStruct((Z // SLABS, R // GROUPS, A), F32),
        in_specs=[VMEM] * 3,
        out_specs=VMEM,
        scratch_shapes=[pltpu.VMEM((A + 16, Z), F32)],
        compiler_params=PARAMS,
        cost_estimate=cost(1 << 29, 4 << 20),
        name="last",
    )(packed, high, low)


def exchange(packed):
    blocks = packed.reshape(SLABS * GROUPS, 4, Z)
    return lax.all_to_all(blocks, ("slab", "freq"), 0, 0, tiled=True).reshape(packed.shape)


def on_device(initial, measured, projector, offsets):
    (angles, angles_low), (even, _), (odd, _) = tables()
    slab = lax.axis_index("slab").astype(jnp.int32)
    group = lax.axis_index("freq").astype(jnp.int32)
    silent = ((slab == 0) & (group == 0)).astype(jnp.int32).reshape(1)
    pieces = lax.all_to_all(arrange(initial, measured), "slab", 0, 0, tiled=True)
    blocks = prepare(slab.reshape(1), projector)
    kept, measured, packed = first_half(offsets, pieces, blocks)
    packed = exchange(middle(exchange(packed), angles, even, odd))
    packed = later_half(silent, offsets, packed, kept, measured, blocks)
    return last(exchange(packed), angles, angles_low)


def solution(mesh):
    placed = (
        P(None, "freq", "slab", None),
        P(None, "freq", "slab", None),
        P(None, None, "freq", None, None),
        P(),
    )
    return jax.shard_map(
        on_device, mesh=mesh, in_specs=placed, out_specs=P("slab", "freq", None), check_vma=False
    )
```

```python
import math

import jax
import jax.numpy as jnp
import numpy as np
from jax import lax
from jax.experimental import pallas as pl
from jax.experimental.pallas import tpu as pltpu
from jax.sharding import PartitionSpec as P

A = 1024
Q = A // 4
STEP_SIZE = 0.25
CLIP_LEVEL = 1.0
SMOOTHING = 0.25
INNER = 2
SLABS = 4
GROUPS = 64
Z = 128
R = 256
F32 = jnp.float32
BF16 = jnp.bfloat16
LEVELS = 32000.0
VMEM = pl.BlockSpec(memory_space=pltpu.VMEM)
SMEM = pl.BlockSpec(memory_space=pltpu.SMEM)
HBM = pl.BlockSpec(memory_space=pltpu.HBM)


def split_table(table):
    high = table.astype(np.float32).astype(jnp.bfloat16)
    low = (table - high.astype(np.float64)).astype(np.float32).astype(jnp.bfloat16)
    return high, low


def tables():
    group, half, part = np.meshgrid(np.arange(GROUPS), np.arange(2), np.arange(2), indexing="ij")
    plain, turned, weights = [], [], []
    for residue in range(4):
        k = (8 * group + residue + 4 * half).reshape(-1)
        imag = part.reshape(-1)[:, None] == 1
        phase = (k[:, None] * np.arange(Q)[None, :] % A) * (2.0 * math.pi / A)
        plain.append(np.where(imag, -np.sin(phase), np.cos(phase)) / math.sqrt(A))
        turned.append(np.where(imag, -np.cos(phase), -np.sin(phase)) / math.sqrt(A))
        weights.append(np.where(k == 0, 1.0, 2.0)[:, None])
    synth = [(p * w).T for p, w in zip(plain, weights)]
    synth_turned = [(t * w).T for t, w in zip(turned, weights)]
    to_angles = np.concatenate(
        [synth[0], synth[2], synth[1], synth_turned[1], synth[3], synth_turned[3]], axis=0
    )
    even = np.concatenate([plain[0], plain[2]], axis=0)
    odd = np.concatenate(
        [np.concatenate([plain[c], turned[c]], axis=1) for c in (1, 3)], axis=0
    )
    return split_table(to_angles), split_table(even), split_table(odd)


def cost(flops, size):
    return pl.CostEstimate(flops=flops, bytes_accessed=size, transcendentals=0)


PARAMS = pltpu.CompilerParams(vmem_limit_bytes=20 << 20)
ALONE = pltpu.CompilerParams(vmem_limit_bytes=100 << 19)
SPECTRUM = jax.ShapeDtypeStruct((2, 2, R, Z), F32)
PACKED = jax.ShapeDtypeStruct((4 * Q, Z), BF16)


def dot(left, right):
    return jnp.dot(left, right, preferred_element_type=F32)


def prepare_kernel(slab_ref, projector_ref, blocks_ref, blocks, sems):
    slab = slab_ref[0]
    loads, stores = [], []
    for half in range(2):
        for part in range(2):
            for slot in range(3):
                copy = pltpu.make_async_copy(
                    projector_ref.at[slot, part, slab + 4 * half],
                    blocks.at[half, 2 + part, :, pl.ds(R * slot, R)],
                    sems.at[len(loads)],
                )
                copy.start()
                loads.append(copy)
    for half in range(2):
        for part in range(2):
            for slot in range(3):
                loads[6 * half + 3 * part + slot].wait()
                cols = pl.ds(R * slot, R)
                blocks[half, part, :, cols] = blocks[half, 2 + part, :, cols].T
        copy = pltpu.make_async_copy(blocks.at[half], blocks_ref.at[half], sems.at[12 + half])
        copy.start()
        stores.append(copy)
    for copy in stores:
        copy.wait()


def prepare(slab, projector):
    return pl.pallas_call(
        prepare_kernel,
        out_shape=jax.ShapeDtypeStruct((4, 4, R, 3 * R), BF16),
        in_specs=[SMEM, HBM],
        out_specs=HBM,
        scratch_shapes=[pltpu.VMEM((2, 4, R, 3 * R), BF16), pltpu.SemaphoreType.DMA((14,))],
        compiler_params=ALONE,
        cost_estimate=cost(0, 8 << 20),
        name="prepare",
    )(slab, projector)


def encode(values):
    largest = jnp.max(jnp.max(jnp.abs(values), axis=1, keepdims=True), axis=0, keepdims=True)
    power = jnp.clip(jnp.ceil(jnp.log2(largest)), -100.0, 100.0)
    return jnp.round(values * (LEVELS * jnp.exp2(-power))).astype(jnp.int32), power


def arrange_kernel(slab_ref, initial_ref, measured_ref, *refs):
    far_refs, (source, pieces, sems) = refs[:SLABS], refs[SLABS:]
    loads, stores = [], []
    for chunk in range(4):
        far = (initial_ref, measured_ref)[chunk // 2].at[chunk % 2]
        loads.append(pltpu.make_async_copy(far, source.at[chunk], sems.at[chunk]))
        loads[-1].start()
    row = lax.broadcasted_iota(jnp.int32, (16, Z), 0)
    heads = [jnp.zeros((16, Z), jnp.int32)] * SLABS
    for chunk in range(4):
        loads[chunk].wait()
        for distance in range(SLABS):
            slab = lax.rem(slab_ref[0] + distance, SLABS)
            for half in range(2):
                block = 2 * chunk + half
                codes, power = encode(source[chunk, slab + 4 * half])
                codes = codes.astype(jnp.int16)
                pieces[distance, pl.ds(64 * block, 32), :] = codes[:, :Z]
                pieces[distance, pl.ds(64 * block + 32, 32), :] = codes[:, Z:]
                heads[distance] = jnp.where(row == block, power.astype(jnp.int32), heads[distance])
    for distance, far in enumerate(far_refs):
        pieces[distance, pl.ds(512, 16), :] = heads[distance].astype(jnp.int16)
        stores.append(pltpu.make_async_copy(pieces.at[distance], far, sems.at[4 + distance]))
        stores[-1].start()
    for copy in stores:
        copy.wait()


def arrange(slab, initial, measured):
    return pl.pallas_call(
        arrange_kernel,
        out_shape=(jax.ShapeDtypeStruct((528, Z), jnp.int16),) * SLABS,
        in_specs=[SMEM, HBM, HBM],
        out_specs=(HBM,) * SLABS,
        scratch_shapes=[
            pltpu.VMEM((4, 2 * SLABS, 32, R), F32),
            pltpu.VMEM((SLABS, 528, Z), jnp.int16),
            pltpu.SemaphoreType.DMA((8,)),
        ],
        compiler_params=pltpu.CompilerParams(vmem_limit_bytes=126 << 19),
        cost_estimate=cost(1 << 20, 1 << 20),
        name="arrange",
    )(slab, initial, measured)


def moved(values, offset, lane):
    source = lane + offset
    rolled = pltpu.roll(values, lax.rem(Z - offset, Z), 1)
    return jnp.where((source >= 0) & (source < Z), rolled, 0.0).astype(BF16)


def swap_blocks(blocks):
    lane = lax.broadcasted_iota(jnp.int32, blocks[0].shape, 1)
    odd32 = (lane // 32) % 2 == 1
    high64 = lane >= 64
    a, b, c, d = blocks
    for_pairs = []
    for low, high in ((a, b), (c, d)):
        for_pairs.append(
            (
                jnp.where(odd32, pltpu.roll(high, 32, 1), low),
                jnp.where(odd32, high, pltpu.roll(low, 96, 1)),
            )
        )
    (a, b), (c, d) = for_pairs
    out = [None] * 4
    for i, (low, high) in enumerate(((a, c), (b, d))):
        out[i] = jnp.where(high64, pltpu.roll(high, 64, 1), low)
        out[i + 2] = jnp.where(high64, high, pltpu.roll(low, 64, 1))
    return out


def slab_rows(slab, index):
    return pl.ds(pl.multiple_of(Q * lax.rem(slab + index, SLABS), Q), Q)


def passes(slab, offsets_ref, blocks_far, iterate, measured, buffers, begin):
    packed_ref, rows_ref, shifted, blocks, sems = buffers
    lane = lax.rem(lax.broadcasted_iota(jnp.int32, (R, Z), 1) + 32 * slab, Z)
    loads = [
        pltpu.make_async_copy(blocks_far.at[half], blocks.at[half], sems.at[half]) for half in range(2)
    ]
    for copy in loads:
        copy.start()

    def place(sign, half, real, imag):
        for slot in range(3):
            rows = pl.ds(R * slot, R)
            offset = sign * offsets_ref[slot]
            shifted[half, rows, :Z] = moved(real, offset, lane)
            shifted[half, rows, Z:] = moved(imag, offset, lane)

    def place_iterate(half):
        place(1, half, iterate[half, 0], iterate[half, 1])

    def product(kind, half):
        by_real = dot(blocks[half, kind], shifted[half])
        by_imag = dot(blocks[half, kind + 1], shifted[half])
        return by_real, by_imag

    def place_residual(half, by_real, by_imag):
        real = measured[half, 0] - (by_real[:, :Z] - by_imag[:, Z:])
        imag = measured[half, 1] - (by_imag[:, :Z] + by_real[:, Z:])
        place(-1, half, real.astype(BF16).astype(F32), imag.astype(BF16).astype(F32))

    def update(half, by_real, by_imag):
        iterate[half, 0] += STEP_SIZE * (by_real[:, :Z] + by_imag[:, Z:])
        iterate[half, 1] += STEP_SIZE * (by_real[:, Z:] - by_imag[:, :Z])

    begin(0)
    begin(1)
    loads[0].wait()
    place_iterate(0)
    place_iterate(1)
    first = product(0, 0)
    loads[1].wait()
    second = product(0, 1)
    for count in range(INNER):
        if count:
            first = product(0, 0)
            second = product(0, 1)
        place_residual(0, *first)
        place_residual(1, *second)
        first = product(2, 0)
        second = product(2, 1)
        update(0, *first)
        update(1, *second)
        if count + 1 < INNER:
            place_iterate(0)
            place_iterate(1)
    pack(0, iterate, rows_ref)
    pack(1, iterate, rows_ref)
    for index in range(SLABS):
        values = rows_ref[pl.ds(Q * index, Q), :].astype(packed_ref.dtype)
        packed_ref[slab_rows(slab, index), :] = values


def pack(half, iterate, rows_ref):
    for part in range(2):
        blocks = [iterate[half, part, pl.ds(i, GROUPS, stride=4), :] for i in range(4)]
        for slab, block in enumerate(swap_blocks(blocks)):
            rows_ref[pl.ds(Q * slab + 2 * half + part, GROUPS, stride=4), :] = block


def first_kernel(
    slab_ref, offsets_ref, own, one, two, three, blocks_far, iterate, measured, packed_ref, column, *scratch
):
    pieces = (own, one, two, three)
    scales = []
    for piece in pieces:
        power = piece[pl.ds(512, 16), :].astype(jnp.int32).astype(F32)
        scales.append(jnp.exp2(power) * (1.0 / LEVELS))

    def begin(half):
        for chunk in range(4):
            block = 2 * chunk + half
            for distance, (piece, scale) in enumerate(zip(pieces, scales)):
                rows = pl.ds(32 * ((SLABS - distance) % SLABS), 32)
                for side in range(2):
                    codes = piece[pl.ds(64 * block + 32 * side, 32), :].astype(jnp.int32)
                    values = codes.astype(F32) * scale[block : block + 1]
                    column[block, rows, Z * side : Z * (side + 1)] = values
            (iterate, measured)[chunk // 2][half, chunk % 2] = column[block].T

    passes(slab_ref[0], offsets_ref, blocks_far, iterate, measured, (packed_ref, *scratch), begin)


def second_kernel(
    slab_ref, silent_ref, offsets_ref, packed_in, kept, measured, blocks_far,
    packed_ref, arrived, iterate, *scratch,
):
    silent = silent_ref[0] != 0
    for index in range(SLABS):
        arrived[pl.ds(Q * index, Q), :] = packed_in[slab_rows(slab_ref[0], index), :].astype(F32)

    def begin(half):
        for part in range(2):
            parts = [
                arrived[pl.ds(Q * slab + 2 * half + part, GROUPS, stride=4), :] for slab in range(4)
            ]
            for i, added in enumerate(swap_blocks(parts)):
                rows = pl.ds(i, GROUPS, stride=4)
                base = kept[half, part, rows, :]
                if half == 0 and part == 1:
                    base = jnp.where(silent, 0.0, base)
                iterate[half, part, rows, :] = base + added

    passes(slab_ref[0], offsets_ref, blocks_far, iterate, measured, (packed_ref, *scratch), begin)


PASS_SCRATCH = [
    pltpu.VMEM((4 * Q, Z), F32),
    pltpu.VMEM((2, 3 * R, 2 * Z), BF16),
    pltpu.VMEM((2, 4, R, 3 * R), BF16),
    pltpu.SemaphoreType.DMA((2,)),
]


def first_half(slab, offsets, pieces, blocks):
    return pl.pallas_call(
        first_kernel,
        out_shape=(SPECTRUM, SPECTRUM, PACKED),
        in_specs=[SMEM, SMEM] + [VMEM] * SLABS + [HBM],
        out_specs=(VMEM,) * 3,
        scratch_shapes=[pltpu.VMEM((8, Z, R), F32)] + PASS_SCRATCH,
        compiler_params=ALONE,
        cost_estimate=cost(2 << 30, 8 << 20),
        name="first_half",
    )(slab, offsets, *pieces, blocks)


def later_half(slab, silent, offsets, packed, kept, measured, blocks):
    return pl.pallas_call(
        second_kernel,
        out_shape=PACKED,
        in_specs=[SMEM] * 3 + [VMEM] * 3 + [HBM],
        out_specs=VMEM,
        scratch_shapes=[pltpu.VMEM((4 * Q, Z), F32), pltpu.VMEM((2, 2, R, Z), F32)] + PASS_SCRATCH,
        compiler_params=ALONE,
        cost_estimate=cost(2 << 30, 8 << 20),
        name="later_half",
    )(slab, silent, offsets, packed, kept, measured, blocks)


def to_volume(packed_ref, tables_ref, volume):
    def residue(c, rows):
        block = packed_ref[pl.ds(Q * c, Q), :]
        total = dot(tables_ref[0][rows, :], block)
        for table in tables_ref[1:]:
            total = total + dot(table[rows, :], block)
        return total

    zero = residue(0, pl.ds(0, Q))
    two = residue(2, pl.ds(Q, Q))
    same, other = zero + two, zero - two
    one = residue(1, pl.ds(2 * Q, 2 * Q))
    three = residue(3, pl.ds(4 * Q, 2 * Q))
    plain = one[:Q] + three[:Q]
    turned = one[Q:] - three[Q:]
    volume[pl.ds(8, Q), :] = same + plain
    volume[pl.ds(8 + Q, Q), :] = other + turned
    volume[pl.ds(8 + 2 * Q, Q), :] = same - plain
    volume[pl.ds(8 + 3 * Q, Q), :] = other - turned
    volume[7:8, :] = volume[A + 7 : A + 8, :]
    volume[A + 8 : A + 9, :] = volume[8:9, :]


def change(volume, start):
    here = volume[pl.ds(8 + start, Q), :]
    before = volume[pl.ds(7 + start, Q), :]
    after = volume[pl.ds(9 + start, Q), :]
    ahead = jnp.clip(after - here, -CLIP_LEVEL, CLIP_LEVEL)
    behind = jnp.clip(here - before, -CLIP_LEVEL, CLIP_LEVEL)
    return here, SMOOTHING * (ahead - behind)


def middle_kernel(packed_ref, angles_ref, even_ref, odd_ref, spectra_ref, volume):
    to_volume(packed_ref, [angles_ref], volume)
    quarters = [change(volume, Q * m)[1] for m in range(4)]
    same, cross = quarters[0] + quarters[2], quarters[1] + quarters[3]
    plain, turned = quarters[0] - quarters[2], quarters[1] - quarters[3]

    def put(c, table, *values):
        values = jnp.concatenate([v.astype(BF16) for v in values], axis=0)
        spectra_ref[pl.ds(Q * c, Q), :] = dot(table, values).astype(spectra_ref.dtype)

    put(0, even_ref[:Q], same + cross)
    put(2, even_ref[Q:], same - cross)
    put(1, odd_ref[:Q], plain, turned)
    put(3, odd_ref[Q:], plain, -turned)


def middle(packed, angles, even, odd):
    return pl.pallas_call(
        middle_kernel,
        out_shape=PACKED,
        in_specs=[VMEM] * 4,
        out_specs=VMEM,
        scratch_shapes=[pltpu.VMEM((A + 16, Z), F32)],
        compiler_params=PARAMS,
        cost_estimate=cost(1 << 30, 4 << 20),
        name="middle",
    )(packed, angles, even, odd)


def last_kernel(packed_ref, high_ref, low_ref, out_ref, volume):
    to_volume(packed_ref, [high_ref, low_ref], volume)
    for m in range(4):
        here, added = change(volume, Q * m)
        values = (here + added).T
        for i in range(4):
            out_ref[:, i, pl.ds(Q * m, Q)] = values[32 * i : 32 * (i + 1), :]


def last(packed, high, low):
    return pl.pallas_call(
        last_kernel,
        out_shape=jax.ShapeDtypeStruct((Z // SLABS, R // GROUPS, A), F32),
        in_specs=[VMEM] * 3,
        out_specs=VMEM,
        scratch_shapes=[pltpu.VMEM((A + 16, Z), F32)],
        compiler_params=PARAMS,
        cost_estimate=cost(1 << 29, 4 << 20),
        name="last",
    )(packed, high, low)


def exchange(packed):
    blocks = packed.reshape(SLABS * GROUPS, 4, Z)
    return lax.all_to_all(blocks, ("slab", "freq"), 0, 0, tiled=True).reshape(packed.shape)


def on_device(initial, measured, projector, offsets):
    (angles, angles_low), (even, _), (odd, _) = tables()
    slab = lax.axis_index("slab").astype(jnp.int32)
    group = lax.axis_index("freq").astype(jnp.int32)
    silent = ((slab == 0) & (group == 0)).astype(jnp.int32).reshape(1)
    slab = slab.reshape(1)
    pieces = list(arrange(slab, initial, measured))
    for distance in range(1, SLABS):
        pairs = [(i, (i + distance) % SLABS) for i in range(SLABS)]
        pieces[distance] = lax.ppermute(pieces[distance], "slab", pairs)
    blocks = prepare(slab, projector)
    kept, measured, packed = first_half(slab, offsets, pieces, blocks)
    packed = exchange(middle(exchange(packed), angles, even, odd))
    packed = later_half(slab, silent, offsets, packed, kept, measured, blocks)
    return last(exchange(packed), angles, angles_low)


def solution(mesh):
    placed = (
        P(None, "freq", "slab", None),
        P(None, "freq", "slab", None),
        P(None, None, "freq", None, None),
        P(),
    )
    return jax.shard_map(
        on_device, mesh=mesh, in_specs=placed, out_specs=P("slab", "freq", None), check_vma=False
    )
```

```python
import math

import jax
import jax.numpy as jnp
import numpy as np
from jax import lax
from jax.experimental import pallas as pl
from jax.experimental.pallas import tpu as pltpu
from jax.sharding import PartitionSpec as P

A = 1024
Q = A // 4
STEP_SIZE = 0.25
CLIP_LEVEL = 1.0
SMOOTHING = 0.25
INNER = 2
SLABS = 4
GROUPS = 64
Z = 128
R = 256
F32 = jnp.float32
BF16 = jnp.bfloat16
LEVELS = 32000.0
VMEM = pl.BlockSpec(memory_space=pltpu.VMEM)
SMEM = pl.BlockSpec(memory_space=pltpu.SMEM)
HBM = pl.BlockSpec(memory_space=pltpu.HBM)


def split_table(table):
    high = table.astype(np.float32).astype(jnp.bfloat16)
    low = (table - high.astype(np.float64)).astype(np.float32).astype(jnp.bfloat16)
    return high, low


def tables():
    group, half, part = np.meshgrid(np.arange(GROUPS), np.arange(2), np.arange(2), indexing="ij")
    plain, turned, weights = [], [], []
    for residue in range(4):
        k = (8 * group + residue + 4 * half).reshape(-1)
        imag = part.reshape(-1)[:, None] == 1
        phase = (k[:, None] * np.arange(Q)[None, :] % A) * (2.0 * math.pi / A)
        plain.append(np.where(imag, -np.sin(phase), np.cos(phase)) / math.sqrt(A))
        turned.append(np.where(imag, -np.cos(phase), -np.sin(phase)) / math.sqrt(A))
        weights.append(np.where(k == 0, 1.0, 2.0)[:, None])
    synth = [(p * w).T for p, w in zip(plain, weights)]
    synth_turned = [(t * w).T for t, w in zip(turned, weights)]
    to_angles = np.concatenate(
        [synth[0], synth[2], synth[1], synth_turned[1], synth[3], synth_turned[3]], axis=0
    )
    even = np.concatenate([plain[0], plain[2]], axis=0)
    odd = np.concatenate(
        [np.concatenate([plain[c], turned[c]], axis=1) for c in (1, 3)], axis=0
    )
    return split_table(to_angles), split_table(even), split_table(odd)


def cost(flops, size):
    return pl.CostEstimate(flops=flops, bytes_accessed=size, transcendentals=0)


PARAMS = pltpu.CompilerParams(vmem_limit_bytes=20 << 20)
ALONE = pltpu.CompilerParams(vmem_limit_bytes=100 << 19)
SPECTRUM = jax.ShapeDtypeStruct((2, 2, R, Z), F32)
PACKED = jax.ShapeDtypeStruct((4 * Q, Z), BF16)


def dot(left, right):
    return jnp.dot(left, right, preferred_element_type=F32)


def prepare_kernel(slab_ref, projector_ref, blocks_ref, blocks, sems):
    slab = slab_ref[0]
    loads, stores = [], []
    for half in range(2):
        for part in range(2):
            for slot in range(3):
                copy = pltpu.make_async_copy(
                    projector_ref.at[slot, part, slab + 4 * half],
                    blocks.at[half, 2 + part, :, pl.ds(R * slot, R)],
                    sems.at[len(loads)],
                )
                copy.start()
                loads.append(copy)
    for half in range(2):
        for part in range(2):
            for slot in range(3):
                loads[6 * half + 3 * part + slot].wait()
                cols = pl.ds(R * slot, R)
                blocks[half, part, :, cols] = blocks[half, 2 + part, :, cols].T
        copy = pltpu.make_async_copy(blocks.at[half], blocks_ref.at[half], sems.at[12 + half])
        copy.start()
        stores.append(copy)
    for copy in stores:
        copy.wait()


def prepare(slab, projector):
    return pl.pallas_call(
        prepare_kernel,
        out_shape=jax.ShapeDtypeStruct((4, 4, R, 3 * R), BF16),
        in_specs=[SMEM, HBM],
        out_specs=HBM,
        scratch_shapes=[pltpu.VMEM((2, 4, R, 3 * R), BF16), pltpu.SemaphoreType.DMA((14,))],
        compiler_params=ALONE,
        cost_estimate=cost(0, 8 << 20),
        name="prepare",
    )(slab, projector)


def encode(values):
    largest = jnp.max(jnp.max(jnp.abs(values), axis=1, keepdims=True), axis=0, keepdims=True)
    power = jnp.clip(jnp.ceil(jnp.log2(largest)), -100.0, 100.0)
    return jnp.round(values * (LEVELS * jnp.exp2(-power))).astype(jnp.int32), power


def arrange_kernel(slab_ref, initial_ref, measured_ref, *piece_refs):
    row = lax.broadcasted_iota(jnp.int32, (16, Z), 0)
    for distance, piece_ref in enumerate(piece_refs):
        slab = lax.rem(slab_ref[0] + distance, SLABS)
        head = jnp.zeros((16, Z), jnp.int32)
        for chunk in range(4):
            source = (initial_ref, measured_ref)[chunk // 2]
            for half in range(2):
                block = 2 * chunk + half
                codes, power = encode(source[chunk % 2, slab + 4 * half])
                codes = codes.astype(jnp.int16)
                piece_ref[pl.ds(64 * block, 32), :] = codes[:, :Z]
                piece_ref[pl.ds(64 * block + 32, 32), :] = codes[:, Z:]
                head = jnp.where(row == block, power.astype(jnp.int32), head)
        piece_ref[pl.ds(512, 16), :] = head.astype(jnp.int16)


def arrange(slab, initial, measured):
    return pl.pallas_call(
        arrange_kernel,
        out_shape=(jax.ShapeDtypeStruct((528, Z), jnp.int16),) * SLABS,
        in_specs=[SMEM, VMEM, VMEM],
        out_specs=(VMEM,) * SLABS,
        compiler_params=ALONE,
        cost_estimate=cost(1 << 20, 1 << 20),
        name="arrange",
    )(slab, initial, measured)


def moved(values, offset, lane):
    source = lane + offset
    rolled = pltpu.roll(values, lax.rem(Z - offset, Z), 1)
    return jnp.where((source >= 0) & (source < Z), rolled, 0.0).astype(BF16)


def swap_blocks(blocks):
    lane = lax.broadcasted_iota(jnp.int32, blocks[0].shape, 1)
    odd32 = (lane // 32) % 2 == 1
    high64 = lane >= 64
    a, b, c, d = blocks
    for_pairs = []
    for low, high in ((a, b), (c, d)):
        for_pairs.append(
            (
                jnp.where(odd32, pltpu.roll(high, 32, 1), low),
                jnp.where(odd32, high, pltpu.roll(low, 96, 1)),
            )
        )
    (a, b), (c, d) = for_pairs
    out = [None] * 4
    for i, (low, high) in enumerate(((a, c), (b, d))):
        out[i] = jnp.where(high64, pltpu.roll(high, 64, 1), low)
        out[i + 2] = jnp.where(high64, high, pltpu.roll(low, 64, 1))
    return out


def slab_rows(slab, index):
    return pl.ds(pl.multiple_of(Q * lax.rem(slab + index, SLABS), Q), Q)


def passes(slab, offsets_ref, blocks_far, iterate, measured, buffers, begin):
    packed_ref, rows_ref, shifted, blocks, sems = buffers
    lane = lax.rem(lax.broadcasted_iota(jnp.int32, (R, Z), 1) + 32 * slab, Z)
    loads = [
        pltpu.make_async_copy(blocks_far.at[half], blocks.at[half], sems.at[half]) for half in range(2)
    ]
    for copy in loads:
        copy.start()

    def place(sign, half, real, imag):
        for slot in range(3):
            rows = pl.ds(R * slot, R)
            offset = sign * offsets_ref[slot]
            shifted[half, rows, :Z] = moved(real, offset, lane)
            shifted[half, rows, Z:] = moved(imag, offset, lane)

    def place_iterate(half):
        place(1, half, iterate[half, 0], iterate[half, 1])

    def product(kind, half):
        by_real = dot(blocks[half, kind], shifted[half])
        by_imag = dot(blocks[half, kind + 1], shifted[half])
        return by_real, by_imag

    def place_residual(half, by_real, by_imag):
        real = measured[half, 0] - (by_real[:, :Z] - by_imag[:, Z:])
        imag = measured[half, 1] - (by_imag[:, :Z] + by_real[:, Z:])
        place(-1, half, real.astype(BF16).astype(F32), imag.astype(BF16).astype(F32))

    def update(half, by_real, by_imag):
        iterate[half, 0] += STEP_SIZE * (by_real[:, :Z] + by_imag[:, Z:])
        iterate[half, 1] += STEP_SIZE * (by_real[:, Z:] - by_imag[:, :Z])

    begin(0)
    begin(1)
    loads[0].wait()
    place_iterate(0)
    place_iterate(1)
    first = product(0, 0)
    loads[1].wait()
    second = product(0, 1)
    for count in range(INNER):
        if count:
            first = product(0, 0)
            second = product(0, 1)
        place_residual(0, *first)
        place_residual(1, *second)
        first = product(2, 0)
        second = product(2, 1)
        update(0, *first)
        update(1, *second)
        if count + 1 < INNER:
            place_iterate(0)
            place_iterate(1)
    pack(0, iterate, rows_ref)
    pack(1, iterate, rows_ref)
    for index in range(SLABS):
        values = rows_ref[pl.ds(Q * index, Q), :].astype(packed_ref.dtype)
        packed_ref[slab_rows(slab, index), :] = values


def pack(half, iterate, rows_ref):
    for part in range(2):
        blocks = [iterate[half, part, pl.ds(i, GROUPS, stride=4), :] for i in range(4)]
        for slab, block in enumerate(swap_blocks(blocks)):
            rows_ref[pl.ds(Q * slab + 2 * half + part, GROUPS, stride=4), :] = block


def first_kernel(
    slab_ref, offsets_ref, own, one, two, three, blocks_far, iterate, measured, packed_ref, column, *scratch
):
    pieces = (own, one, two, three)
    scales = []
    for piece in pieces:
        power = piece[pl.ds(512, 16), :].astype(jnp.int32).astype(F32)
        scales.append(jnp.exp2(power) * (1.0 / LEVELS))

    def begin(half):
        for chunk in range(4):
            block = 2 * chunk + half
            for distance, (piece, scale) in enumerate(zip(pieces, scales)):
                rows = pl.ds(32 * ((SLABS - distance) % SLABS), 32)
                for side in range(2):
                    codes = piece[pl.ds(64 * block + 32 * side, 32), :].astype(jnp.int32)
                    values = codes.astype(F32) * scale[block : block + 1]
                    column[block, rows, Z * side : Z * (side + 1)] = values
            (iterate, measured)[chunk // 2][half, chunk % 2] = column[block].T

    passes(slab_ref[0], offsets_ref, blocks_far, iterate, measured, (packed_ref, *scratch), begin)


def second_kernel(
    slab_ref, silent_ref, offsets_ref, packed_in, kept, measured, blocks_far,
    packed_ref, arrived, iterate, *scratch,
):
    silent = silent_ref[0] != 0
    for index in range(SLABS):
        arrived[pl.ds(Q * index, Q), :] = packed_in[slab_rows(slab_ref[0], index), :].astype(F32)

    def begin(half):
        for part in range(2):
            parts = [
                arrived[pl.ds(Q * slab + 2 * half + part, GROUPS, stride=4), :] for slab in range(4)
            ]
            for i, added in enumerate(swap_blocks(parts)):
                rows = pl.ds(i, GROUPS, stride=4)
                base = kept[half, part, rows, :]
                if half == 0 and part == 1:
                    base = jnp.where(silent, 0.0, base)
                iterate[half, part, rows, :] = base + added

    passes(slab_ref[0], offsets_ref, blocks_far, iterate, measured, (packed_ref, *scratch), begin)


PASS_SCRATCH = [
    pltpu.VMEM((4 * Q, Z), F32),
    pltpu.VMEM((2, 3 * R, 2 * Z), BF16),
    pltpu.VMEM((2, 4, R, 3 * R), BF16),
    pltpu.SemaphoreType.DMA((2,)),
]


def first_half(slab, offsets, pieces, blocks):
    return pl.pallas_call(
        first_kernel,
        out_shape=(SPECTRUM, SPECTRUM, PACKED),
        in_specs=[SMEM, SMEM] + [VMEM] * SLABS + [HBM],
        out_specs=(VMEM,) * 3,
        scratch_shapes=[pltpu.VMEM((8, Z, R), F32)] + PASS_SCRATCH,
        compiler_params=ALONE,
        cost_estimate=cost(2 << 30, 8 << 20),
        name="first_half",
    )(slab, offsets, *pieces, blocks)


def later_half(slab, silent, offsets, packed, kept, measured, blocks):
    return pl.pallas_call(
        second_kernel,
        out_shape=PACKED,
        in_specs=[SMEM] * 3 + [VMEM] * 3 + [HBM],
        out_specs=VMEM,
        scratch_shapes=[pltpu.VMEM((4 * Q, Z), F32), pltpu.VMEM((2, 2, R, Z), F32)] + PASS_SCRATCH,
        compiler_params=ALONE,
        cost_estimate=cost(2 << 30, 8 << 20),
        name="later_half",
    )(slab, silent, offsets, packed, kept, measured, blocks)


def to_volume(packed_ref, tables_ref, volume):
    def residue(c, rows):
        block = packed_ref[pl.ds(Q * c, Q), :]
        total = dot(tables_ref[0][rows, :], block)
        for table in tables_ref[1:]:
            total = total + dot(table[rows, :], block)
        return total

    if len(tables_ref) == 1:
        one, three = residue(1, pl.ds(2 * Q, Q)), residue(3, pl.ds(4 * Q, Q))
        plain = one + three
        zero, two = residue(0, pl.ds(0, Q)), residue(2, pl.ds(Q, Q))
        same = zero + two
        volume[pl.ds(8, Q), :] = same + plain
        volume[pl.ds(8 + 2 * Q, Q), :] = same - plain
        other = zero - two
        turned = residue(1, pl.ds(3 * Q, Q)) - residue(3, pl.ds(5 * Q, Q))
        volume[pl.ds(8 + Q, Q), :] = other + turned
        volume[pl.ds(8 + 3 * Q, Q), :] = other - turned
    else:
        zero = residue(0, pl.ds(0, Q))
        two = residue(2, pl.ds(Q, Q))
        same, other = zero + two, zero - two
        one = residue(1, pl.ds(2 * Q, 2 * Q))
        three = residue(3, pl.ds(4 * Q, 2 * Q))
        plain = one[:Q] + three[:Q]
        turned = one[Q:] - three[Q:]
        volume[pl.ds(8, Q), :] = same + plain
        volume[pl.ds(8 + Q, Q), :] = other + turned
        volume[pl.ds(8 + 2 * Q, Q), :] = same - plain
        volume[pl.ds(8 + 3 * Q, Q), :] = other - turned
    volume[7:8, :] = volume[A + 7 : A + 8, :]
    volume[A + 8 : A + 9, :] = volume[8:9, :]


def change(volume, start):
    here = volume[pl.ds(8 + start, Q), :]
    before = volume[pl.ds(7 + start, Q), :]
    after = volume[pl.ds(9 + start, Q), :]
    ahead = jnp.clip(after - here, -CLIP_LEVEL, CLIP_LEVEL)
    behind = jnp.clip(here - before, -CLIP_LEVEL, CLIP_LEVEL)
    return here, SMOOTHING * (ahead - behind)


def middle_kernel(packed_ref, angles_ref, even_ref, odd_ref, spectra_ref, volume):
    to_volume(packed_ref, [angles_ref], volume)
    quarters = [change(volume, Q * m)[1] for m in range(4)]
    same, cross = quarters[0] + quarters[2], quarters[1] + quarters[3]
    plain, turned = quarters[0] - quarters[2], quarters[1] - quarters[3]

    def put(c, table, *values):
        values = jnp.concatenate([v.astype(BF16) for v in values], axis=0)
        spectra_ref[pl.ds(Q * c, Q), :] = dot(table, values).astype(spectra_ref.dtype)

    put(0, even_ref[:Q], same + cross)
    put(2, even_ref[Q:], same - cross)
    put(1, odd_ref[:Q], plain, turned)
    put(3, odd_ref[Q:], plain, -turned)


def middle(packed, angles, even, odd):
    return pl.pallas_call(
        middle_kernel,
        out_shape=PACKED,
        in_specs=[VMEM] * 4,
        out_specs=VMEM,
        scratch_shapes=[pltpu.VMEM((A + 16, Z), F32)],
        compiler_params=PARAMS,
        cost_estimate=cost(1 << 30, 4 << 20),
        name="middle",
    )(packed, angles, even, odd)


def last_kernel(packed_ref, high_ref, low_ref, out_ref, volume):
    to_volume(packed_ref, [high_ref, low_ref], volume)
    for m in range(4):
        here, added = change(volume, Q * m)
        values = (here + added).T
        for i in range(4):
            out_ref[:, i, pl.ds(Q * m, Q)] = values[32 * i : 32 * (i + 1), :]


def last(packed, high, low):
    return pl.pallas_call(
        last_kernel,
        out_shape=jax.ShapeDtypeStruct((Z // SLABS, R // GROUPS, A), F32),
        in_specs=[VMEM] * 3,
        out_specs=VMEM,
        scratch_shapes=[pltpu.VMEM((A + 16, Z), F32)],
        compiler_params=PARAMS,
        cost_estimate=cost(1 << 29, 4 << 20),
        name="last",
    )(packed, high, low)


def exchange(packed):
    blocks = packed.reshape(SLABS * GROUPS, 4, Z)
    return lax.all_to_all(blocks, ("slab", "freq"), 0, 0, tiled=True).reshape(packed.shape)


def on_device(initial, measured, projector, offsets):
    (angles, angles_low), (even, _), (odd, _) = tables()
    slab = lax.axis_index("slab").astype(jnp.int32)
    group = lax.axis_index("freq").astype(jnp.int32)
    silent = ((slab == 0) & (group == 0)).astype(jnp.int32).reshape(1)
    slab = slab.reshape(1)
    pieces = list(arrange(slab, initial, measured))
    for distance in range(1, SLABS):
        pairs = [(i, (i + distance) % SLABS) for i in range(SLABS)]
        pieces[distance] = lax.ppermute(pieces[distance], "slab", pairs)
    blocks = prepare(slab, projector)
    kept, measured, packed = first_half(slab, offsets, pieces, blocks)
    packed = exchange(middle(exchange(packed), angles, even, odd))
    packed = later_half(slab, silent, offsets, packed, kept, measured, blocks)
    return last(exchange(packed), angles, angles_low)


def solution(mesh):
    placed = (
        P(None, "freq", "slab", None),
        P(None, "freq", "slab", None),
        P(None, None, "freq", None, None),
        P(),
    )
    return jax.shard_map(
        on_device, mesh=mesh, in_specs=placed, out_specs=P("slab", "freq", None), check_vma=False
    )
```

```python
import math

import jax
import jax.numpy as jnp
import numpy as np
from jax import lax
from jax.experimental import pallas as pl
from jax.experimental.pallas import tpu as pltpu
from jax.sharding import PartitionSpec as P

A = 1024
Q = A // 4
STEP_SIZE = 0.25
CLIP_LEVEL = 1.0
SMOOTHING = 0.25
INNER = 2
SLABS = 4
GROUPS = 64
Z = 128
R = 256
F32 = jnp.float32
BF16 = jnp.bfloat16
LEVELS = 32000.0
VMEM = pl.BlockSpec(memory_space=pltpu.VMEM)
SMEM = pl.BlockSpec(memory_space=pltpu.SMEM)
HBM = pl.BlockSpec(memory_space=pltpu.HBM)


def split_table(table):
    high = table.astype(np.float32).astype(jnp.bfloat16)
    low = (table - high.astype(np.float64)).astype(np.float32).astype(jnp.bfloat16)
    return high, low


def tables():
    group, half, part = np.meshgrid(np.arange(GROUPS), np.arange(2), np.arange(2), indexing="ij")
    plain, turned, weights = [], [], []
    for residue in range(4):
        k = (8 * group + residue + 4 * half).reshape(-1)
        imag = part.reshape(-1)[:, None] == 1
        phase = (k[:, None] * np.arange(Q)[None, :] % A) * (2.0 * math.pi / A)
        plain.append(np.where(imag, -np.sin(phase), np.cos(phase)) / math.sqrt(A))
        turned.append(np.where(imag, -np.cos(phase), -np.sin(phase)) / math.sqrt(A))
        weights.append(np.where(k == 0, 1.0, 2.0)[:, None])
    synth = [(p * w).T for p, w in zip(plain, weights)]
    synth_turned = [(t * w).T for t, w in zip(turned, weights)]
    to_angles = np.concatenate(
        [synth[0], synth[2], synth[1], synth_turned[1], synth[3], synth_turned[3]], axis=0
    )
    even = np.concatenate([plain[0], plain[2]], axis=0)
    odd = np.concatenate(
        [np.concatenate([plain[c], turned[c]], axis=1) for c in (1, 3)], axis=0
    )
    return split_table(to_angles), split_table(even), split_table(odd)


def cost(flops, size):
    return pl.CostEstimate(flops=flops, bytes_accessed=size, transcendentals=0)


PARAMS = pltpu.CompilerParams(vmem_limit_bytes=20 << 20)
ALONE = pltpu.CompilerParams(vmem_limit_bytes=100 << 19)
SPECTRUM = jax.ShapeDtypeStruct((2, 2, R, Z), F32)
PACKED = jax.ShapeDtypeStruct((4 * Q, Z), BF16)


def dot(left, right):
    return jnp.dot(left, right, preferred_element_type=F32)


def prepare_kernel(slab_ref, projector_ref, turned_ref, plain_0, plain_far, plain_ref, sems):
    slab = slab_ref[0]
    loads, stores = [], []
    for half in range(2):
        for part in range(2):
            for slot in range(3):
                copy = pltpu.make_async_copy(
                    projector_ref.at[slot, part, slab + 4 * half],
                    plain_ref.at[half, part, :, pl.ds(R * slot, R)],
                    sems.at[len(loads)],
                )
                copy.start()
                loads.append(copy)
    for half in range(2):
        for part in range(2):
            for slot in range(3):
                loads[6 * half + 3 * part + slot].wait()
                cols = pl.ds(R * slot, R)
                turned_ref[half, part, :, cols] = plain_ref[half, part, :, cols].T
        if half == 0:
            plain_0[...] = plain_ref[0]
        copy = pltpu.make_async_copy(plain_ref.at[half], plain_far.at[half], sems.at[12 + half])
        copy.start()
        stores.append(copy)
    for copy in stores:
        copy.wait()


def prepare(slab, projector):
    blocks = jax.ShapeDtypeStruct((2, 2, R, 3 * R), BF16)
    return pl.pallas_call(
        prepare_kernel,
        out_shape=(
            blocks,
            jax.ShapeDtypeStruct(blocks.shape[1:], BF16),
            jax.ShapeDtypeStruct((16, 2, R, 3 * R), BF16),
        ),
        in_specs=[SMEM, HBM],
        out_specs=(VMEM, VMEM, HBM),
        scratch_shapes=[pltpu.VMEM(blocks.shape, BF16), pltpu.SemaphoreType.DMA((14,))],
        compiler_params=pltpu.CompilerParams(vmem_limit_bytes=100 << 19),
        cost_estimate=cost(0, 8 << 20),
        name="prepare",
    )(slab, projector)


def encode(values):
    largest = jnp.max(jnp.max(jnp.abs(values), axis=1, keepdims=True), axis=0, keepdims=True)
    power = jnp.clip(jnp.ceil(jnp.log2(largest)), -100.0, 100.0)
    return jnp.round(values * (LEVELS * jnp.exp2(-power))).astype(jnp.int32), power


def arrange_kernel(slab_ref, initial_ref, measured_ref, *piece_refs):
    row = lax.broadcasted_iota(jnp.int32, (16, Z), 0)
    for distance, piece_ref in enumerate(piece_refs):
        slab = lax.rem(slab_ref[0] + distance, SLABS)
        head = jnp.zeros((16, Z), jnp.int32)
        for chunk in range(4):
            source = (initial_ref, measured_ref)[chunk // 2]
            for half in range(2):
                block = 2 * chunk + half
                codes, power = encode(source[chunk % 2, slab + 4 * half])
                codes = codes.astype(jnp.int16)
                piece_ref[pl.ds(64 * block, 32), :] = codes[:, :Z]
                piece_ref[pl.ds(64 * block + 32, 32), :] = codes[:, Z:]
                head = jnp.where(row == block, power.astype(jnp.int32), head)
        piece_ref[pl.ds(512, 16), :] = head.astype(jnp.int16)


def arrange(slab, initial, measured):
    return pl.pallas_call(
        arrange_kernel,
        out_shape=(jax.ShapeDtypeStruct((528, Z), jnp.int16),) * SLABS,
        in_specs=[SMEM, VMEM, VMEM],
        out_specs=(VMEM,) * SLABS,
        compiler_params=ALONE,
        cost_estimate=cost(1 << 20, 1 << 20),
        name="arrange",
    )(slab, initial, measured)


def moved(values, offset, lane):
    source = lane + offset
    rolled = pltpu.roll(values, lax.rem(Z - offset, Z), 1)
    return jnp.where((source >= 0) & (source < Z), rolled, 0.0).astype(BF16)


def swap_blocks(blocks):
    lane = lax.broadcasted_iota(jnp.int32, blocks[0].shape, 1)
    odd32 = (lane // 32) % 2 == 1
    high64 = lane >= 64
    a, b, c, d = blocks
    for_pairs = []
    for low, high in ((a, b), (c, d)):
        for_pairs.append(
            (
                jnp.where(odd32, pltpu.roll(high, 32, 1), low),
                jnp.where(odd32, high, pltpu.roll(low, 96, 1)),
            )
        )
    (a, b), (c, d) = for_pairs
    out = [None] * 4
    for i, (low, high) in enumerate(((a, c), (b, d))):
        out[i] = jnp.where(high64, pltpu.roll(high, 64, 1), low)
        out[i + 2] = jnp.where(high64, high, pltpu.roll(low, 64, 1))
    return out


def slab_rows(slab, index):
    return pl.ds(pl.multiple_of(Q * lax.rem(slab + index, SLABS), Q), Q)


def passes(slab, offsets_ref, turned, plain, iterate, measured, buffers, begin, waits=None):
    packed_ref, rows_ref, shifted = buffers
    waits = waits or {}
    lane = lax.rem(lax.broadcasted_iota(jnp.int32, (R, Z), 1) + 32 * slab, Z)
    def place(sign, half, real, imag):
        for slot in range(3):
            rows = pl.ds(R * slot, R)
            offset = sign * offsets_ref[slot]
            shifted[half, rows, :Z] = moved(real, offset, lane)
            shifted[half, rows, Z:] = moved(imag, offset, lane)

    def place_iterate(half):
        place(1, half, iterate[half, 0], iterate[half, 1])

    def product(blocks, half):
        return [dot(blocks[half][part], shifted[half]) for part in range(2)]

    def place_residual(half, by_real, by_imag):
        real = measured[half, 0] - (by_real[:, :Z] - by_imag[:, Z:])
        imag = measured[half, 1] - (by_imag[:, :Z] + by_real[:, Z:])
        place(-1, half, real.astype(BF16).astype(F32), imag.astype(BF16).astype(F32))

    def update(half, by_real, by_imag):
        iterate[half, 0] += STEP_SIZE * (by_real[:, :Z] + by_imag[:, Z:])
        iterate[half, 1] += STEP_SIZE * (by_real[:, Z:] - by_imag[:, :Z])

    begin(0)
    begin(1)
    place_iterate(0)
    place_iterate(1)
    first = product(turned, 0)
    second = product(turned, 1)
    for count in range(INNER):
        if count:
            first = product(turned, 0)
            second = product(turned, 1)
        for copy in waits.pop(0, ()):
            copy.wait()
        place_residual(0, *first)
        place_residual(1, *second)
        first = product(plain, 0)
        for copy in waits.pop(1, ()):
            copy.wait()
        second = product(plain, 1)
        update(0, *first)
        update(1, *second)
        if count + 1 < INNER:
            place_iterate(0)
            place_iterate(1)
    pack(0, iterate, rows_ref)
    pack(1, iterate, rows_ref)
    for index in range(SLABS):
        values = rows_ref[pl.ds(Q * index, Q), :].astype(packed_ref.dtype)
        packed_ref[slab_rows(slab, index), :] = values


def pack(half, iterate, rows_ref):
    for part in range(2):
        blocks = [iterate[half, part, pl.ds(i, GROUPS, stride=4), :] for i in range(4)]
        for slab, block in enumerate(swap_blocks(blocks)):
            rows_ref[pl.ds(Q * slab + 2 * half + part, GROUPS, stride=4), :] = block


def first_kernel(
    slab_ref, offsets_ref, own, one, two, three, turned, plain_0, plain_far,
    iterate, measured_far, packed_ref, column, measured, plain_1, sems, *scratch,
):
    load = pltpu.make_async_copy(plain_far.at[1], plain_1, sems.at[1])
    load.start()
    pieces = (own, one, two, three)
    scales = []
    for piece in pieces:
        power = piece[pl.ds(512, 16), :].astype(jnp.int32).astype(F32)
        scales.append(jnp.exp2(power) * (1.0 / LEVELS))

    def begin(half):
        for chunk in range(4):
            block = 2 * chunk + half
            for distance, (piece, scale) in enumerate(zip(pieces, scales)):
                rows = pl.ds(32 * ((SLABS - distance) % SLABS), 32)
                for side in range(2):
                    codes = piece[pl.ds(64 * block + 32 * side, 32), :].astype(jnp.int32)
                    values = codes.astype(F32) * scale[block : block + 1]
                    column[block, rows, Z * side : Z * (side + 1)] = values
            (iterate, measured)[chunk // 2][half, chunk % 2] = column[block].T
        if half:
            store.start()

    store = pltpu.make_async_copy(measured, measured_far.at[pl.ds(0, 2)], sems.at[0])
    turned = [turned.at[half] for half in range(2)]
    buffers = (packed_ref, *scratch)
    waits = {1: [load]}
    passes(
        slab_ref[0], offsets_ref, turned, [plain_0, plain_1], iterate, measured, buffers, begin, waits
    )
    store.wait()


def second_kernel(
    slab_ref, silent_ref, offsets_ref, packed_in, kept, measured_far, turned, plain_far,
    packed_ref, arrived, iterate, measured, plain, sems, *scratch,
):
    loads = [pltpu.make_async_copy(measured_far.at[pl.ds(0, 2)], measured, sems.at[0])]
    for half in range(2):
        loads.append(pltpu.make_async_copy(plain_far.at[half], plain.at[half], sems.at[1 + half]))
    for copy in loads:
        copy.start()
    silent = silent_ref[0] != 0
    for index in range(SLABS):
        arrived[pl.ds(Q * index, Q), :] = packed_in[slab_rows(slab_ref[0], index), :].astype(F32)

    def begin(half):
        for part in range(2):
            parts = [
                arrived[pl.ds(Q * slab + 2 * half + part, GROUPS, stride=4), :] for slab in range(4)
            ]
            for i, added in enumerate(swap_blocks(parts)):
                rows = pl.ds(i, GROUPS, stride=4)
                base = kept[half, part, rows, :]
                if half == 0 and part == 1:
                    base = jnp.where(silent, 0.0, base)
                iterate[half, part, rows, :] = base + added

    buffers = (packed_ref, *scratch)
    waits = {0: loads[:2], 1: loads[2:]}
    turned, plain = [[blocks.at[half] for half in range(2)] for blocks in (turned, plain)]
    passes(slab_ref[0], offsets_ref, turned, plain, iterate, measured, buffers, begin, waits)


PASS_SCRATCH = [
    pltpu.VMEM((4 * Q, Z), F32),
    pltpu.VMEM((2, 3 * R, 2 * Z), BF16),
]


def first_half(slab, offsets, pieces, turned, plain_0, plain_far):
    return pl.pallas_call(
        first_kernel,
        out_shape=(SPECTRUM, jax.ShapeDtypeStruct((48, 2, R, Z), F32), PACKED),
        in_specs=[SMEM, SMEM] + [VMEM] * (SLABS + 2) + [HBM],
        out_specs=(VMEM, HBM, VMEM),
        scratch_shapes=[
            pltpu.VMEM((8, Z, R), F32),
            pltpu.VMEM((2, 2, R, Z), F32),
            pltpu.VMEM((2, R, 3 * R), BF16),
            pltpu.SemaphoreType.DMA((2,)),
        ]
        + PASS_SCRATCH,
        compiler_params=ALONE,
        cost_estimate=cost(2 << 30, 8 << 20),
        name="first_half",
    )(slab, offsets, *pieces, turned, plain_0, plain_far)


def later_half(slab, silent, offsets, packed, kept, measured, turned, plain):
    return pl.pallas_call(
        second_kernel,
        out_shape=PACKED,
        in_specs=[SMEM] * 3 + [VMEM, VMEM, HBM, VMEM, HBM],
        out_specs=VMEM,
        scratch_shapes=[
            pltpu.VMEM((4 * Q, Z), F32),
            pltpu.VMEM((2, 2, R, Z), F32),
            pltpu.VMEM((2, 2, R, Z), F32),
            pltpu.VMEM((2, 2, R, 3 * R), BF16),
            pltpu.SemaphoreType.DMA((3,)),
        ]
        + PASS_SCRATCH,
        compiler_params=ALONE,
        cost_estimate=cost(2 << 30, 8 << 20),
        name="later_half",
    )(slab, silent, offsets, packed, kept, measured, turned, plain)


def to_volume(packed_ref, tables_ref, volume):
    def residue(c, rows):
        block = packed_ref[pl.ds(Q * c, Q), :]
        total = dot(tables_ref[0][rows, :], block)
        for table in tables_ref[1:]:
            total = total + dot(table[rows, :], block)
        return total

    if len(tables_ref) == 1:
        one, three = residue(1, pl.ds(2 * Q, Q)), residue(3, pl.ds(4 * Q, Q))
        plain = one + three
        zero, two = residue(0, pl.ds(0, Q)), residue(2, pl.ds(Q, Q))
        same = zero + two
        volume[pl.ds(8, Q), :] = same + plain
        volume[pl.ds(8 + 2 * Q, Q), :] = same - plain
        other = zero - two
        turned = residue(1, pl.ds(3 * Q, Q)) - residue(3, pl.ds(5 * Q, Q))
        volume[pl.ds(8 + Q, Q), :] = other + turned
        volume[pl.ds(8 + 3 * Q, Q), :] = other - turned
    else:
        zero = residue(0, pl.ds(0, Q))
        two = residue(2, pl.ds(Q, Q))
        same, other = zero + two, zero - two
        one = residue(1, pl.ds(2 * Q, 2 * Q))
        three = residue(3, pl.ds(4 * Q, 2 * Q))
        plain = one[:Q] + three[:Q]
        turned = one[Q:] - three[Q:]
        volume[pl.ds(8, Q), :] = same + plain
        volume[pl.ds(8 + Q, Q), :] = other + turned
        volume[pl.ds(8 + 2 * Q, Q), :] = same - plain
        volume[pl.ds(8 + 3 * Q, Q), :] = other - turned
    volume[7:8, :] = volume[A + 7 : A + 8, :]
    volume[A + 8 : A + 9, :] = volume[8:9, :]


def change(volume, start):
    here = volume[pl.ds(8 + start, Q), :]
    before = volume[pl.ds(7 + start, Q), :]
    after = volume[pl.ds(9 + start, Q), :]
    ahead = jnp.clip(after - here, -CLIP_LEVEL, CLIP_LEVEL)
    behind = jnp.clip(here - before, -CLIP_LEVEL, CLIP_LEVEL)
    return here, SMOOTHING * (ahead - behind)


def middle_kernel(packed_ref, angles_ref, even_ref, odd_ref, spectra_ref, volume):
    to_volume(packed_ref, [angles_ref], volume)
    quarters = [change(volume, Q * m)[1] for m in range(4)]
    same, cross = quarters[0] + quarters[2], quarters[1] + quarters[3]
    plain, turned = quarters[0] - quarters[2], quarters[1] - quarters[3]

    def put(c, table, *values):
        values = jnp.concatenate([v.astype(BF16) for v in values], axis=0)
        spectra_ref[pl.ds(Q * c, Q), :] = dot(table, values).astype(spectra_ref.dtype)

    put(0, even_ref[:Q], same + cross)
    put(2, even_ref[Q:], same - cross)
    put(1, odd_ref[:Q], plain, turned)
    put(3, odd_ref[Q:], plain, -turned)


def middle(packed, angles, even, odd):
    return pl.pallas_call(
        middle_kernel,
        out_shape=PACKED,
        in_specs=[VMEM] * 4,
        out_specs=VMEM,
        scratch_shapes=[pltpu.VMEM((A + 16, Z), F32)],
        compiler_params=PARAMS,
        cost_estimate=cost(1 << 30, 4 << 20),
        name="middle",
    )(packed, angles, even, odd)


def last_kernel(packed_ref, high_ref, low_ref, out_ref, volume):
    to_volume(packed_ref, [high_ref, low_ref], volume)
    for m in range(4):
        here, added = change(volume, Q * m)
        values = (here + added).T
        for i in range(4):
            out_ref[:, i, pl.ds(Q * m, Q)] = values[32 * i : 32 * (i + 1), :]


def last(packed, high, low):
    return pl.pallas_call(
        last_kernel,
        out_shape=jax.ShapeDtypeStruct((Z // SLABS, R // GROUPS, A), F32),
        in_specs=[VMEM] * 3,
        out_specs=VMEM,
        scratch_shapes=[pltpu.VMEM((A + 16, Z), F32)],
        compiler_params=PARAMS,
        cost_estimate=cost(1 << 29, 4 << 20),
        name="last",
    )(packed, high, low)


def exchange(packed):
    blocks = packed.reshape(SLABS * GROUPS, 4, Z)
    return lax.all_to_all(blocks, ("slab", "freq"), 0, 0, tiled=True).reshape(packed.shape)


def on_device(initial, measured, projector, offsets):
    (angles, angles_low), (even, _), (odd, _) = tables()
    slab = lax.axis_index("slab").astype(jnp.int32)
    group = lax.axis_index("freq").astype(jnp.int32)
    silent = ((slab == 0) & (group == 0)).astype(jnp.int32).reshape(1)
    slab = slab.reshape(1)
    pieces = list(arrange(slab, initial, measured))
    for distance in range(1, SLABS):
        pairs = [(i, (i + distance) % SLABS) for i in range(SLABS)]
        pieces[distance] = lax.ppermute(pieces[distance], "slab", pairs)
    turned, plain_0, plain_far = prepare(slab, projector)
    kept, measured, packed = first_half(slab, offsets, pieces, turned, plain_0, plain_far)
    packed = exchange(middle(exchange(packed), angles, even, odd))
    packed = later_half(slab, silent, offsets, packed, kept, measured, turned, plain_far)
    return last(exchange(packed), angles, angles_low)


def solution(mesh):
    placed = (
        P(None, "freq", "slab", None),
        P(None, "freq", "slab", None),
        P(None, None, "freq", None, None),
        P(),
    )
    return jax.shard_map(
        on_device, mesh=mesh, in_specs=placed, out_specs=P("slab", "freq", None), check_vma=False
    )
```

```python
import math

import jax
import jax.numpy as jnp
import numpy as np
from jax import lax
from jax.experimental import pallas as pl
from jax.experimental.pallas import tpu as pltpu
from jax.sharding import PartitionSpec as P

A = 1024
Q = A // 4
STEP_SIZE = 0.25
CLIP_LEVEL = 1.0
SMOOTHING = 0.25
INNER = 2
SLABS = 4
GROUPS = 64
Z = 128
R = 256
F32 = jnp.float32
BF16 = jnp.bfloat16
LEVELS = 32000.0
VMEM = pl.BlockSpec(memory_space=pltpu.VMEM)
SMEM = pl.BlockSpec(memory_space=pltpu.SMEM)
HBM = pl.BlockSpec(memory_space=pltpu.HBM)


def split_table(table):
    high = table.astype(np.float32).astype(jnp.bfloat16)
    low = (table - high.astype(np.float64)).astype(np.float32).astype(jnp.bfloat16)
    return high, low


def tables():
    group, half, part = np.meshgrid(np.arange(GROUPS), np.arange(2), np.arange(2), indexing="ij")
    plain, turned, weights = [], [], []
    for residue in range(4):
        k = (8 * group + residue + 4 * half).reshape(-1)
        imag = part.reshape(-1)[:, None] == 1
        phase = (k[:, None] * np.arange(Q)[None, :] % A) * (2.0 * math.pi / A)
        plain.append(np.where(imag, -np.sin(phase), np.cos(phase)) / math.sqrt(A))
        turned.append(np.where(imag, -np.cos(phase), -np.sin(phase)) / math.sqrt(A))
        weights.append(np.where(k == 0, 1.0, 2.0)[:, None])
    synth = [(p * w).T for p, w in zip(plain, weights)]
    synth_turned = [(t * w).T for t, w in zip(turned, weights)]
    to_angles = np.concatenate(
        [synth[0], synth[2], synth[1], synth_turned[1], synth[3], synth_turned[3]], axis=0
    )
    even = np.concatenate([plain[0], plain[2]], axis=0)
    odd = np.concatenate(
        [np.concatenate([plain[c], turned[c]], axis=1) for c in (1, 3)], axis=0
    )
    return split_table(to_angles), split_table(even), split_table(odd)


def cost(flops, size):
    return pl.CostEstimate(flops=flops, bytes_accessed=size, transcendentals=0)


PARAMS = pltpu.CompilerParams(vmem_limit_bytes=20 << 20)
ALONE = pltpu.CompilerParams(vmem_limit_bytes=100 << 19)
HALF = pltpu.CompilerParams(
    vmem_limit_bytes=100 << 19
)
SPECTRUM = jax.ShapeDtypeStruct((2, 2, R, Z), F32)
PACKED = jax.ShapeDtypeStruct((4 * Q, Z), BF16)


def dot(left, right):
    return jnp.dot(left, right, preferred_element_type=F32)


def prepare_kernel(
    slab_ref, offsets_ref, projector_ref, turned_ref, plain_0, plain_far, near_ref, plain_ref, sems
):
    slab = slab_ref[0]
    for slot in range(3):
        near_ref[slot] = offsets_ref[slot]
    loads, stores = [], []
    for half in range(2):
        for part in range(2):
            for slot in range(3):
                copy = pltpu.make_async_copy(
                    projector_ref.at[slot, part, slab + 4 * half],
                    plain_ref.at[half, part, :, pl.ds(R * slot, R)],
                    sems.at[len(loads)],
                )
                copy.start()
                loads.append(copy)
    for half in range(2):
        for part in range(2):
            for slot in range(3):
                loads[6 * half + 3 * part + slot].wait()
                cols = pl.ds(R * slot, R)
                turned_ref[half, part, :, cols] = plain_ref[half, part, :, cols].T
        if half == 0:
            plain_0[...] = plain_ref[0]
        copy = pltpu.make_async_copy(plain_ref.at[half], plain_far.at[half], sems.at[12 + half])
        copy.start()
        stores.append(copy)
    for copy in stores:
        copy.wait()


def prepare(slab, offsets, projector):
    blocks = jax.ShapeDtypeStruct((2, 2, R, 3 * R), BF16)
    return pl.pallas_call(
        prepare_kernel,
        out_shape=(
            blocks,
            jax.ShapeDtypeStruct(blocks.shape[1:], BF16),
            jax.ShapeDtypeStruct((16, 2, R, 3 * R), BF16),
            jax.ShapeDtypeStruct((3,), jnp.int32),
        ),
        in_specs=[SMEM, SMEM, HBM],
        out_specs=(VMEM, VMEM, HBM, SMEM),
        scratch_shapes=[pltpu.VMEM(blocks.shape, BF16), pltpu.SemaphoreType.DMA((14,))],
        compiler_params=pltpu.CompilerParams(vmem_limit_bytes=100 << 19),
        cost_estimate=cost(0, 8 << 20),
        name="prepare",
    )(slab, offsets, projector)


def encode(values):
    largest = jnp.max(jnp.max(jnp.abs(values), axis=1, keepdims=True), axis=0, keepdims=True)
    power = jnp.clip(jnp.ceil(jnp.log2(largest)), -100.0, 100.0)
    return jnp.round(values * (LEVELS * jnp.exp2(-power))).astype(jnp.int32), power


def arrange_kernel(slab_ref, initial_ref, measured_ref, *piece_refs):
    row = lax.broadcasted_iota(jnp.int32, (16, Z), 0)
    for distance, piece_ref in enumerate(piece_refs):
        slab = lax.rem(slab_ref[0] + distance, SLABS)
        head = jnp.zeros((16, Z), jnp.int32)
        for chunk in range(4):
            source = (initial_ref, measured_ref)[chunk // 2]
            for half in range(2):
                block = 2 * chunk + half
                codes, power = encode(source[chunk % 2, slab + 4 * half])
                codes = codes.astype(jnp.int16)
                piece_ref[pl.ds(64 * block, 32), :] = codes[:, :Z]
                piece_ref[pl.ds(64 * block + 32, 32), :] = codes[:, Z:]
                head = jnp.where(row == block, power.astype(jnp.int32), head)
        piece_ref[pl.ds(512, 16), :] = head.astype(jnp.int16)


def arrange(slab, initial, measured):
    return pl.pallas_call(
        arrange_kernel,
        out_shape=(jax.ShapeDtypeStruct((528, Z), jnp.int16),) * SLABS,
        in_specs=[SMEM, VMEM, VMEM],
        out_specs=(VMEM,) * SLABS,
        compiler_params=ALONE,
        cost_estimate=cost(1 << 20, 1 << 20),
        name="arrange",
    )(slab, initial, measured)


def moved(values, offset, lane):
    source = lane + offset
    rolled = pltpu.roll(values, lax.rem(Z - offset, Z), 1)
    return jnp.where((source >= 0) & (source < Z), rolled, 0.0).astype(BF16)


def swap_blocks(blocks):
    lane = lax.broadcasted_iota(jnp.int32, blocks[0].shape, 1)
    odd32 = (lane // 32) % 2 == 1
    high64 = lane >= 64
    a, b, c, d = blocks
    for_pairs = []
    for low, high in ((a, b), (c, d)):
        for_pairs.append(
            (
                jnp.where(odd32, pltpu.roll(high, 32, 1), low),
                jnp.where(odd32, high, pltpu.roll(low, 96, 1)),
            )
        )
    (a, b), (c, d) = for_pairs
    out = [None] * 4
    for i, (low, high) in enumerate(((a, c), (b, d))):
        out[i] = jnp.where(high64, pltpu.roll(high, 64, 1), low)
        out[i + 2] = jnp.where(high64, high, pltpu.roll(low, 64, 1))
    return out


def slab_rows(slab, index):
    return pl.ds(pl.multiple_of(Q * lax.rem(slab + index, SLABS), Q), Q)


def passes(slab, offsets_ref, turned, plain, iterate, measured, buffers, begin, waits=None):
    packed_ref, rows_ref, shifted = buffers
    waits = waits or {}
    lane = lax.rem(lax.broadcasted_iota(jnp.int32, (R, Z), 1) + 32 * slab, Z)
    def place(sign, half, real, imag):
        for slot in range(3):
            rows = pl.ds(R * slot, R)
            offset = sign * offsets_ref[slot]
            shifted[half, rows, :Z] = moved(real, offset, lane)
            shifted[half, rows, Z:] = moved(imag, offset, lane)

    def place_iterate(half):
        place(1, half, iterate[half, 0], iterate[half, 1])

    def product(blocks, half):
        return [dot(blocks[half][part], shifted[half]) for part in range(2)]

    def place_residual(half, by_real, by_imag):
        real = measured[half, 0] - (by_real[:, :Z] - by_imag[:, Z:])
        imag = measured[half, 1] - (by_imag[:, :Z] + by_real[:, Z:])
        place(-1, half, real.astype(BF16).astype(F32), imag.astype(BF16).astype(F32))

    def update(half, by_real, by_imag):
        iterate[half, 0] += STEP_SIZE * (by_real[:, :Z] + by_imag[:, Z:])
        iterate[half, 1] += STEP_SIZE * (by_real[:, Z:] - by_imag[:, :Z])

    begin(0)
    begin(1)
    place_iterate(0)
    place_iterate(1)
    first = product(turned, 0)
    second = product(turned, 1)
    for count in range(INNER):
        if count:
            first = product(turned, 0)
            second = product(turned, 1)
        for copy in waits.pop(0, ()):
            copy.wait()
        place_residual(0, *first)
        place_residual(1, *second)
        first = product(plain, 0)
        for copy in waits.pop(1, ()):
            copy.wait()
        second = product(plain, 1)
        update(0, *first)
        update(1, *second)
        if count + 1 < INNER:
            place_iterate(0)
            place_iterate(1)
    pack(0, iterate, rows_ref)
    pack(1, iterate, rows_ref)
    for index in range(SLABS):
        values = rows_ref[pl.ds(Q * index, Q), :].astype(packed_ref.dtype)
        packed_ref[slab_rows(slab, index), :] = values


def pack(half, iterate, rows_ref):
    for part in range(2):
        blocks = [iterate[half, part, pl.ds(i, GROUPS, stride=4), :] for i in range(4)]
        for slab, block in enumerate(swap_blocks(blocks)):
            rows_ref[pl.ds(Q * slab + 2 * half + part, GROUPS, stride=4), :] = block


def first_kernel(
    slab_ref, offsets_ref, own, one, two, three, turned, plain_0, plain_far,
    iterate, measured_far, packed_ref, column, measured, plain_1, sems, *scratch,
):
    load = pltpu.make_async_copy(plain_far.at[1], plain_1, sems.at[1])
    load.start()
    pieces = (own, one, two, three)
    scales = []
    for piece in pieces:
        power = piece[pl.ds(512, 16), :].astype(jnp.int32).astype(F32)
        scales.append(jnp.exp2(power) * (1.0 / LEVELS))

    def begin(half):
        for chunk in range(4):
            block = 2 * chunk + half
            for distance, (piece, scale) in enumerate(zip(pieces, scales)):
                rows = pl.ds(32 * ((SLABS - distance) % SLABS), 32)
                for side in range(2):
                    codes = piece[pl.ds(64 * block + 32 * side, 32), :].astype(jnp.int32)
                    values = codes.astype(F32) * scale[block : block + 1]
                    column[block, rows, Z * side : Z * (side + 1)] = values
            (iterate, measured)[chunk // 2][half, chunk % 2] = column[block].T
        if half:
            store.start()

    store = pltpu.make_async_copy(measured, measured_far.at[pl.ds(0, 2)], sems.at[0])
    turned = [turned.at[half] for half in range(2)]
    buffers = (packed_ref, *scratch)
    waits = {1: [load]}
    passes(
        slab_ref[0], offsets_ref, turned, [plain_0, plain_1], iterate, measured, buffers, begin, waits
    )
    store.wait()


def second_kernel(
    slab_ref, silent_ref, offsets_ref, packed_in, kept, measured_far, turned, plain_far,
    packed_ref, arrived, iterate, measured, plain, sems, *scratch,
):
    loads = [pltpu.make_async_copy(measured_far.at[pl.ds(0, 2)], measured, sems.at[0])]
    for half in range(2):
        loads.append(pltpu.make_async_copy(plain_far.at[half], plain.at[half], sems.at[1 + half]))
    for copy in loads:
        copy.start()
    silent = silent_ref[0] != 0
    for index in range(SLABS):
        arrived[pl.ds(Q * index, Q), :] = packed_in[slab_rows(slab_ref[0], index), :].astype(F32)

    def begin(half):
        for part in range(2):
            parts = [
                arrived[pl.ds(Q * slab + 2 * half + part, GROUPS, stride=4), :] for slab in range(4)
            ]
            for i, added in enumerate(swap_blocks(parts)):
                rows = pl.ds(i, GROUPS, stride=4)
                base = kept[half, part, rows, :]
                if half == 0 and part == 1:
                    base = jnp.where(silent, 0.0, base)
                iterate[half, part, rows, :] = base + added

    buffers = (packed_ref, *scratch)
    waits = {0: loads[:2], 1: loads[2:]}
    turned, plain = [[blocks.at[half] for half in range(2)] for blocks in (turned, plain)]
    passes(slab_ref[0], offsets_ref, turned, plain, iterate, measured, buffers, begin, waits)


PASS_SCRATCH = [
    pltpu.VMEM((4 * Q, Z), F32),
    pltpu.VMEM((2, 3 * R, 2 * Z), BF16),
]


def first_half(slab, offsets, pieces, turned, plain_0, plain_far):
    return pl.pallas_call(
        first_kernel,
        out_shape=(SPECTRUM, jax.ShapeDtypeStruct((48, 2, R, Z), F32), PACKED),
        in_specs=[SMEM, SMEM] + [VMEM] * (SLABS + 2) + [HBM],
        out_specs=(VMEM, HBM, VMEM),
        scratch_shapes=[
            pltpu.VMEM((8, Z, R), F32),
            pltpu.VMEM((2, 2, R, Z), F32),
            pltpu.VMEM((2, R, 3 * R), BF16),
            pltpu.SemaphoreType.DMA((2,)),
        ]
        + PASS_SCRATCH,
        compiler_params=HALF,
        cost_estimate=cost(2 << 30, 8 << 20),
        name="first_half",
    )(slab, offsets, *pieces, turned, plain_0, plain_far)


def later_half(slab, silent, offsets, packed, kept, measured, turned, plain):
    return pl.pallas_call(
        second_kernel,
        out_shape=PACKED,
        in_specs=[SMEM] * 3 + [VMEM, VMEM, HBM, VMEM, HBM],
        out_specs=VMEM,
        scratch_shapes=[
            pltpu.VMEM((4 * Q, Z), F32),
            pltpu.VMEM((2, 2, R, Z), F32),
            pltpu.VMEM((2, 2, R, Z), F32),
            pltpu.VMEM((2, 2, R, 3 * R), BF16),
            pltpu.SemaphoreType.DMA((3,)),
        ]
        + PASS_SCRATCH,
        compiler_params=HALF,
        cost_estimate=cost(2 << 30, 8 << 20),
        name="later_half",
    )(slab, silent, offsets, packed, kept, measured, turned, plain)


def to_volume(packed_ref, tables_ref, volume):
    def residue(c, rows):
        block = packed_ref[pl.ds(Q * c, Q), :]
        total = dot(tables_ref[0][rows, :], block)
        for table in tables_ref[1:]:
            total = total + dot(table[rows, :], block)
        return total

    if len(tables_ref) == 1:
        one, three = residue(1, pl.ds(2 * Q, Q)), residue(3, pl.ds(4 * Q, Q))
        plain = one + three
        zero, two = residue(0, pl.ds(0, Q)), residue(2, pl.ds(Q, Q))
        same = zero + two
        volume[pl.ds(8, Q), :] = same + plain
        volume[pl.ds(8 + 2 * Q, Q), :] = same - plain
        other = zero - two
        turned = residue(1, pl.ds(3 * Q, Q)) - residue(3, pl.ds(5 * Q, Q))
        volume[pl.ds(8 + Q, Q), :] = other + turned
        volume[pl.ds(8 + 3 * Q, Q), :] = other - turned
    else:
        zero = residue(0, pl.ds(0, Q))
        two = residue(2, pl.ds(Q, Q))
        same, other = zero + two, zero - two
        one = residue(1, pl.ds(2 * Q, 2 * Q))
        three = residue(3, pl.ds(4 * Q, 2 * Q))
        plain = one[:Q] + three[:Q]
        turned = one[Q:] - three[Q:]
        volume[pl.ds(8, Q), :] = same + plain
        volume[pl.ds(8 + Q, Q), :] = other + turned
        volume[pl.ds(8 + 2 * Q, Q), :] = same - plain
        volume[pl.ds(8 + 3 * Q, Q), :] = other - turned
    volume[7:8, :] = volume[A + 7 : A + 8, :]
    volume[A + 8 : A + 9, :] = volume[8:9, :]


def change(volume, start):
    here = volume[pl.ds(8 + start, Q), :]
    before = volume[pl.ds(7 + start, Q), :]
    after = volume[pl.ds(9 + start, Q), :]
    ahead = jnp.clip(after - here, -CLIP_LEVEL, CLIP_LEVEL)
    behind = jnp.clip(here - before, -CLIP_LEVEL, CLIP_LEVEL)
    return here, SMOOTHING * (ahead - behind)


def middle_kernel(packed_ref, angles_ref, even_ref, odd_ref, spectra_ref, volume):
    to_volume(packed_ref, [angles_ref], volume)
    quarters = [change(volume, Q * m)[1] for m in range(4)]
    same, cross = quarters[0] + quarters[2], quarters[1] + quarters[3]
    plain, turned = quarters[0] - quarters[2], quarters[1] - quarters[3]

    def put(c, table, *values):
        values = jnp.concatenate([v.astype(BF16) for v in values], axis=0)
        spectra_ref[pl.ds(Q * c, Q), :] = dot(table, values).astype(spectra_ref.dtype)

    put(0, even_ref[:Q], same + cross)
    put(2, even_ref[Q:], same - cross)
    put(1, odd_ref[:Q], plain, turned)
    put(3, odd_ref[Q:], plain, -turned)


def middle(packed, angles, even, odd):
    return pl.pallas_call(
        middle_kernel,
        out_shape=PACKED,
        in_specs=[VMEM] * 4,
        out_specs=VMEM,
        scratch_shapes=[pltpu.VMEM((A + 16, Z), F32)],
        compiler_params=PARAMS,
        cost_estimate=cost(1 << 30, 4 << 20),
        name="middle",
    )(packed, angles, even, odd)


def last_kernel(packed_ref, high_ref, low_ref, out_ref, volume):
    to_volume(packed_ref, [high_ref, low_ref], volume)
    for m in range(4):
        here, added = change(volume, Q * m)
        values = (here + added).T
        for i in range(4):
            out_ref[:, i, pl.ds(Q * m, Q)] = values[32 * i : 32 * (i + 1), :]


def last(packed, high, low):
    return pl.pallas_call(
        last_kernel,
        out_shape=jax.ShapeDtypeStruct((Z // SLABS, R // GROUPS, A), F32),
        in_specs=[VMEM] * 3,
        out_specs=VMEM,
        scratch_shapes=[pltpu.VMEM((A + 16, Z), F32)],
        compiler_params=PARAMS,
        cost_estimate=cost(1 << 29, 4 << 20),
        name="last",
    )(packed, high, low)


def exchange(packed):
    blocks = packed.reshape(SLABS * GROUPS, 4, Z)
    return lax.all_to_all(blocks, ("slab", "freq"), 0, 0, tiled=True).reshape(packed.shape)


def on_device(initial, measured, projector, offsets):
    (angles, angles_low), (even, _), (odd, _) = tables()
    slab = lax.axis_index("slab").astype(jnp.int32)
    group = lax.axis_index("freq").astype(jnp.int32)
    silent = ((slab == 0) & (group == 0)).astype(jnp.int32).reshape(1)
    slab = slab.reshape(1)
    pieces = list(arrange(slab, initial, measured))
    for distance in range(1, SLABS):
        pairs = [(i, (i + distance) % SLABS) for i in range(SLABS)]
        pieces[distance] = lax.ppermute(pieces[distance], "slab", pairs)
    turned, plain_0, plain_far, offsets = prepare(slab, offsets, projector)
    kept, measured, packed = first_half(slab, offsets, pieces, turned, plain_0, plain_far)
    packed = exchange(middle(exchange(packed), angles, even, odd))
    packed = later_half(slab, silent, offsets, packed, kept, measured, turned, plain_far)
    return last(exchange(packed), angles, angles_low)


def solution(mesh):
    placed = (
        P(None, "freq", "slab", None),
        P(None, "freq", "slab", None),
        P(None, None, "freq", None, None),
        P(),
    )
    return jax.shard_map(
        on_device, mesh=mesh, in_specs=placed, out_specs=P("slab", "freq", None), check_vma=False
    )
```

```python
import math

import jax
import jax.numpy as jnp
import numpy as np
from jax import lax
from jax.experimental import pallas as pl
from jax.experimental.pallas import tpu as pltpu
from jax.sharding import PartitionSpec as P

A = 1024
Q = A // 4
STEP_SIZE = 0.25
CLIP_LEVEL = 1.0
SMOOTHING = 0.25
INNER = 2
SLABS = 4
GROUPS = 64
Z = 128
R = 256
F32 = jnp.float32
BF16 = jnp.bfloat16
LEVELS = 32000.0
VMEM = pl.BlockSpec(memory_space=pltpu.VMEM)
SMEM = pl.BlockSpec(memory_space=pltpu.SMEM)
HBM = pl.BlockSpec(memory_space=pltpu.HBM)


def split_table(table):
    high = table.astype(np.float32).astype(jnp.bfloat16)
    low = (table - high.astype(np.float64)).astype(np.float32).astype(jnp.bfloat16)
    return high, low


def tables():
    group, half, part = np.meshgrid(np.arange(GROUPS), np.arange(2), np.arange(2), indexing="ij")
    plain, turned, weights = [], [], []
    for residue in range(4):
        k = (8 * group + residue + 4 * half).reshape(-1)
        imag = part.reshape(-1)[:, None] == 1
        phase = (k[:, None] * np.arange(Q)[None, :] % A) * (2.0 * math.pi / A)
        plain.append(np.where(imag, -np.sin(phase), np.cos(phase)) / math.sqrt(A))
        turned.append(np.where(imag, -np.cos(phase), -np.sin(phase)) / math.sqrt(A))
        weights.append(np.where(k == 0, 1.0, 2.0)[:, None])
    synth = [(p * w).T for p, w in zip(plain, weights)]
    synth_turned = [(t * w).T for t, w in zip(turned, weights)]
    to_angles = np.concatenate(
        [synth[0], synth[2], synth[1], synth_turned[1], synth[3], synth_turned[3]], axis=0
    )
    even = np.concatenate([plain[0], plain[2]], axis=0)
    odd = np.concatenate(
        [np.concatenate([plain[c], turned[c]], axis=1) for c in (1, 3)], axis=0
    )
    return split_table(to_angles), split_table(even), split_table(odd)


def cost(flops, size):
    return pl.CostEstimate(flops=flops, bytes_accessed=size, transcendentals=0)


PARAMS = pltpu.CompilerParams(vmem_limit_bytes=20 << 20)
ALONE = pltpu.CompilerParams(vmem_limit_bytes=100 << 19)
HALF = pltpu.CompilerParams(
    vmem_limit_bytes=100 << 19
)
SPECTRUM = jax.ShapeDtypeStruct((2, 2, R, Z), F32)
PACKED = jax.ShapeDtypeStruct((4 * Q, Z), BF16)


def dot(left, right):
    return jnp.dot(left, right, preferred_element_type=F32)


def prepare_kernel(
    slab_ref, offsets_ref, projector_ref, turned_ref, plain_0, plain_far, near_ref, plain_ref, sems
):
    slab = slab_ref[0]
    for slot in range(3):
        near_ref[slot] = offsets_ref[slot]
    loads, stores = [], []
    for half in range(2):
        for part in range(2):
            for slot in range(3):
                copy = pltpu.make_async_copy(
                    projector_ref.at[slot, part, slab + 4 * half],
                    plain_ref.at[half, part, :, pl.ds(R * slot, R)],
                    sems.at[len(loads)],
                )
                copy.start()
                loads.append(copy)
    for half in range(2):
        for part in range(2):
            for slot in range(3):
                loads[6 * half + 3 * part + slot].wait()
                cols = pl.ds(R * slot, R)
                turned_ref[half, part, :, cols] = plain_ref[half, part, :, cols].T
        if half == 0:
            plain_0[...] = plain_ref[0]
        copy = pltpu.make_async_copy(plain_ref.at[half], plain_far.at[half], sems.at[12 + half])
        copy.start()
        stores.append(copy)
    for copy in stores:
        copy.wait()


def prepare(slab, offsets, projector):
    blocks = jax.ShapeDtypeStruct((2, 2, R, 3 * R), BF16)
    return pl.pallas_call(
        prepare_kernel,
        out_shape=(
            blocks,
            jax.ShapeDtypeStruct(blocks.shape[1:], BF16),
            jax.ShapeDtypeStruct((16, 2, R, 3 * R), BF16),
            jax.ShapeDtypeStruct((3,), jnp.int32),
        ),
        in_specs=[SMEM, SMEM, HBM],
        out_specs=(VMEM, VMEM, HBM, SMEM),
        scratch_shapes=[pltpu.VMEM(blocks.shape, BF16), pltpu.SemaphoreType.DMA((14,))],
        compiler_params=pltpu.CompilerParams(vmem_limit_bytes=100 << 19),
        cost_estimate=cost(0, 8 << 20),
        name="prepare",
    )(slab, offsets, projector)


def encode(values):
    largest = jnp.max(jnp.max(jnp.abs(values), axis=1, keepdims=True), axis=0, keepdims=True)
    power = jnp.clip(jnp.ceil(jnp.log2(largest)), -100.0, 100.0)
    return jnp.round(values * (LEVELS * jnp.exp2(-power))).astype(jnp.int32), power


def arrange_kernel(slab_ref, initial_ref, measured_ref, *piece_refs):
    row = lax.broadcasted_iota(jnp.int32, (16, Z), 0)
    for distance, piece_ref in enumerate(piece_refs):
        slab = lax.rem(slab_ref[0] + distance, SLABS)
        head = jnp.zeros((16, Z), jnp.int32)
        for chunk in range(4):
            source = (initial_ref, measured_ref)[chunk // 2]
            for half in range(2):
                block = 2 * chunk + half
                codes, power = encode(source[chunk % 2, slab + 4 * half])
                codes = codes.astype(jnp.int16)
                piece_ref[pl.ds(64 * block, 32), :] = codes[:, :Z]
                piece_ref[pl.ds(64 * block + 32, 32), :] = codes[:, Z:]
                head = jnp.where(row == block, power.astype(jnp.int32), head)
        piece_ref[pl.ds(512, 16), :] = head.astype(jnp.int16)


def arrange(slab, initial, measured):
    return pl.pallas_call(
        arrange_kernel,
        out_shape=(jax.ShapeDtypeStruct((528, Z), jnp.int16),) * SLABS,
        in_specs=[SMEM, VMEM, VMEM],
        out_specs=(VMEM,) * SLABS,
        compiler_params=ALONE,
        cost_estimate=cost(1 << 20, 1 << 20),
        name="arrange",
    )(slab, initial, measured)


def moved(values, offset, lane):
    source = lane + offset
    rolled = pltpu.roll(values, lax.rem(Z - offset, Z), 1)
    return jnp.where((source >= 0) & (source < Z), rolled, 0.0).astype(BF16)


def swap_blocks(blocks):
    lane = lax.broadcasted_iota(jnp.int32, blocks[0].shape, 1)
    odd32 = (lane // 32) % 2 == 1
    high64 = lane >= 64
    a, b, c, d = blocks
    for_pairs = []
    for low, high in ((a, b), (c, d)):
        for_pairs.append(
            (
                jnp.where(odd32, pltpu.roll(high, 32, 1), low),
                jnp.where(odd32, high, pltpu.roll(low, 96, 1)),
            )
        )
    (a, b), (c, d) = for_pairs
    out = [None] * 4
    for i, (low, high) in enumerate(((a, c), (b, d))):
        out[i] = jnp.where(high64, pltpu.roll(high, 64, 1), low)
        out[i + 2] = jnp.where(high64, high, pltpu.roll(low, 64, 1))
    return out


def slab_rows(slab, index):
    return pl.ds(pl.multiple_of(Q * lax.rem(slab + index, SLABS), Q), Q)


def passes(slab, offsets_ref, turned, plain, iterate, measured, buffers, begin, waits=None):
    packed_ref, rows_ref, shifted = buffers
    waits = waits or {}
    lane = lax.rem(lax.broadcasted_iota(jnp.int32, (R, Z), 1) + 32 * slab, Z)
    def place(sign, half, real, imag):
        for slot in range(3):
            rows = pl.ds(R * slot, R)
            offset = sign * offsets_ref[slot]
            shifted[half, rows, :Z] = moved(real, offset, lane)
            shifted[half, rows, Z:] = moved(imag, offset, lane)

    def place_iterate(half):
        place(1, half, iterate[half, 0], iterate[half, 1])

    def product(blocks, half):
        return [dot(blocks[half][part], shifted[half]) for part in range(2)]

    def place_residual(half, by_real, by_imag):
        real = measured[half, 0] - (by_real[:, :Z] - by_imag[:, Z:])
        imag = measured[half, 1] - (by_imag[:, :Z] + by_real[:, Z:])
        place(-1, half, real.astype(BF16).astype(F32), imag.astype(BF16).astype(F32))

    def update(half, by_real, by_imag):
        iterate[half, 0] += STEP_SIZE * (by_real[:, :Z] + by_imag[:, Z:])
        iterate[half, 1] += STEP_SIZE * (by_real[:, Z:] - by_imag[:, :Z])

    begin(0)
    begin(1)
    place_iterate(0)
    place_iterate(1)
    first = product(turned, 0)
    second = product(turned, 1)
    for count in range(INNER):
        if count:
            first = product(turned, 0)
            second = product(turned, 1)
        for copy in waits.pop(0, ()):
            copy.wait()
        place_residual(0, *first)
        place_residual(1, *second)
        for copy in waits.pop(1, ()):
            copy.wait()
        first = product(plain, 0)
        for copy in waits.pop(2, ()):
            copy.wait()
        second = product(plain, 1)
        update(0, *first)
        update(1, *second)
        if count + 1 < INNER:
            place_iterate(0)
            place_iterate(1)
    pack(0, iterate, rows_ref)
    pack(1, iterate, rows_ref)
    for index in range(SLABS):
        values = rows_ref[pl.ds(Q * index, Q), :].astype(packed_ref.dtype)
        packed_ref[slab_rows(slab, index), :] = values


def pack(half, iterate, rows_ref):
    for part in range(2):
        blocks = [iterate[half, part, pl.ds(i, GROUPS, stride=4), :] for i in range(4)]
        for slab, block in enumerate(swap_blocks(blocks)):
            rows_ref[pl.ds(Q * slab + 2 * half + part, GROUPS, stride=4), :] = block


def first_kernel(
    slab_ref, offsets_ref, own, one, two, three, turned, plain_0, plain_far,
    iterate, measured_far, packed_ref, column, measured, plain_1, sems, *scratch,
):
    load = pltpu.make_async_copy(plain_far.at[1], plain_1, sems.at[1])
    load.start()
    pieces = (own, one, two, three)
    scales = []
    for piece in pieces:
        power = piece[pl.ds(512, 16), :].astype(jnp.int32).astype(F32)
        scales.append(jnp.exp2(power) * (1.0 / LEVELS))

    def begin(half):
        for chunk in range(4):
            block = 2 * chunk + half
            for distance, (piece, scale) in enumerate(zip(pieces, scales)):
                rows = pl.ds(32 * ((SLABS - distance) % SLABS), 32)
                for side in range(2):
                    codes = piece[pl.ds(64 * block + 32 * side, 32), :].astype(jnp.int32)
                    values = codes.astype(F32) * scale[block : block + 1]
                    column[block, rows, Z * side : Z * (side + 1)] = values
            (iterate, measured)[chunk // 2][half, chunk % 2] = column[block].T
        if half:
            store.start()

    store = pltpu.make_async_copy(measured, measured_far.at[pl.ds(0, 2)], sems.at[0])
    turned = [turned.at[half] for half in range(2)]
    buffers = (packed_ref, *scratch)
    waits = {2: [load]}
    passes(
        slab_ref[0], offsets_ref, turned, [plain_0, plain_1], iterate, measured, buffers, begin, waits
    )
    store.wait()


def second_kernel(
    slab_ref, silent_ref, offsets_ref, packed_in, kept, measured_far, turned, plain_far,
    packed_ref, arrived, iterate, measured, plain, sems, *scratch,
):
    loads = [pltpu.make_async_copy(measured_far.at[pl.ds(0, 2)], measured, sems.at[0])]
    for half in range(2):
        loads.append(pltpu.make_async_copy(plain_far.at[half], plain.at[half], sems.at[1 + half]))
    for copy in loads:
        copy.start()
    silent = silent_ref[0] != 0
    for index in range(SLABS):
        arrived[pl.ds(Q * index, Q), :] = packed_in[slab_rows(slab_ref[0], index), :].astype(F32)

    def begin(half):
        for part in range(2):
            parts = [
                arrived[pl.ds(Q * slab + 2 * half + part, GROUPS, stride=4), :] for slab in range(4)
            ]
            for i, added in enumerate(swap_blocks(parts)):
                rows = pl.ds(i, GROUPS, stride=4)
                base = kept[half, part, rows, :]
                if half == 0 and part == 1:
                    base = jnp.where(silent, 0.0, base)
                iterate[half, part, rows, :] = base + added

    buffers = (packed_ref, *scratch)
    waits = {0: loads[:1], 1: loads[1:2], 2: loads[2:]}
    turned, plain = [[blocks.at[half] for half in range(2)] for blocks in (turned, plain)]
    passes(slab_ref[0], offsets_ref, turned, plain, iterate, measured, buffers, begin, waits)


PASS_SCRATCH = [
    pltpu.VMEM((4 * Q, Z), F32),
    pltpu.VMEM((2, 3 * R, 2 * Z), BF16),
]


def first_half(slab, offsets, pieces, turned, plain_0, plain_far):
    return pl.pallas_call(
        first_kernel,
        out_shape=(SPECTRUM, jax.ShapeDtypeStruct((48, 2, R, Z), F32), PACKED),
        in_specs=[SMEM, SMEM] + [VMEM] * (SLABS + 2) + [HBM],
        out_specs=(VMEM, HBM, VMEM),
        scratch_shapes=[
            pltpu.VMEM((8, Z, R), F32),
            pltpu.VMEM((2, 2, R, Z), F32),
            pltpu.VMEM((2, R, 3 * R), BF16),
            pltpu.SemaphoreType.DMA((2,)),
        ]
        + PASS_SCRATCH,
        compiler_params=HALF,
        cost_estimate=cost(2 << 30, 8 << 20),
        name="first_half",
    )(slab, offsets, *pieces, turned, plain_0, plain_far)


def later_half(slab, silent, offsets, packed, kept, measured, turned, plain):
    return pl.pallas_call(
        second_kernel,
        out_shape=PACKED,
        in_specs=[SMEM] * 3 + [VMEM, VMEM, HBM, VMEM, HBM],
        out_specs=VMEM,
        scratch_shapes=[
            pltpu.VMEM((4 * Q, Z), F32),
            pltpu.VMEM((2, 2, R, Z), F32),
            pltpu.VMEM((2, 2, R, Z), F32),
            pltpu.VMEM((2, 2, R, 3 * R), BF16),
            pltpu.SemaphoreType.DMA((3,)),
        ]
        + PASS_SCRATCH,
        compiler_params=HALF,
        cost_estimate=cost(2 << 30, 8 << 20),
        name="later_half",
    )(slab, silent, offsets, packed, kept, measured, turned, plain)


def to_volume(packed_ref, tables_ref, volume):
    def residue(c, rows):
        block = packed_ref[pl.ds(Q * c, Q), :]
        total = dot(tables_ref[0][rows, :], block)
        for table in tables_ref[1:]:
            total = total + dot(table[rows, :], block)
        return total

    if len(tables_ref) == 1:
        one, three = residue(1, pl.ds(2 * Q, Q)), residue(3, pl.ds(4 * Q, Q))
        plain = one + three
        zero, two = residue(0, pl.ds(0, Q)), residue(2, pl.ds(Q, Q))
        same = zero + two
        volume[pl.ds(8, Q), :] = same + plain
        volume[pl.ds(8 + 2 * Q, Q), :] = same - plain
        other = zero - two
        turned = residue(1, pl.ds(3 * Q, Q)) - residue(3, pl.ds(5 * Q, Q))
        volume[pl.ds(8 + Q, Q), :] = other + turned
        volume[pl.ds(8 + 3 * Q, Q), :] = other - turned
    else:
        zero = residue(0, pl.ds(0, Q))
        two = residue(2, pl.ds(Q, Q))
        same, other = zero + two, zero - two
        one = residue(1, pl.ds(2 * Q, 2 * Q))
        three = residue(3, pl.ds(4 * Q, 2 * Q))
        plain = one[:Q] + three[:Q]
        turned = one[Q:] - three[Q:]
        volume[pl.ds(8, Q), :] = same + plain
        volume[pl.ds(8 + Q, Q), :] = other + turned
        volume[pl.ds(8 + 2 * Q, Q), :] = same - plain
        volume[pl.ds(8 + 3 * Q, Q), :] = other - turned
    volume[7:8, :] = volume[A + 7 : A + 8, :]
    volume[A + 8 : A + 9, :] = volume[8:9, :]


def change(volume, start):
    here = volume[pl.ds(8 + start, Q), :]
    before = volume[pl.ds(7 + start, Q), :]
    after = volume[pl.ds(9 + start, Q), :]
    ahead = jnp.clip(after - here, -CLIP_LEVEL, CLIP_LEVEL)
    behind = jnp.clip(here - before, -CLIP_LEVEL, CLIP_LEVEL)
    return here, SMOOTHING * (ahead - behind)


def middle_kernel(packed_ref, angles_ref, even_ref, odd_ref, spectra_ref, volume):
    to_volume(packed_ref, [angles_ref], volume)
    quarters = [change(volume, Q * m)[1] for m in range(4)]
    same, cross = quarters[0] + quarters[2], quarters[1] + quarters[3]
    plain, turned = quarters[0] - quarters[2], quarters[1] - quarters[3]

    def put(c, table, *values):
        values = jnp.concatenate([v.astype(BF16) for v in values], axis=0)
        spectra_ref[pl.ds(Q * c, Q), :] = dot(table, values).astype(spectra_ref.dtype)

    put(0, even_ref[:Q], same + cross)
    put(2, even_ref[Q:], same - cross)
    put(1, odd_ref[:Q], plain, turned)
    put(3, odd_ref[Q:], plain, -turned)


def middle(packed, angles, even, odd):
    return pl.pallas_call(
        middle_kernel,
        out_shape=PACKED,
        in_specs=[VMEM] * 4,
        out_specs=VMEM,
        scratch_shapes=[pltpu.VMEM((A + 16, Z), F32)],
        compiler_params=PARAMS,
        cost_estimate=cost(1 << 30, 4 << 20),
        name="middle",
    )(packed, angles, even, odd)


def last_kernel(packed_ref, high_ref, low_ref, out_ref, volume):
    to_volume(packed_ref, [high_ref, low_ref], volume)
    for m in range(4):
        here, added = change(volume, Q * m)
        values = (here + added).T
        for i in range(4):
            out_ref[:, i, pl.ds(Q * m, Q)] = values[32 * i : 32 * (i + 1), :]


def last(packed, high, low):
    return pl.pallas_call(
        last_kernel,
        out_shape=jax.ShapeDtypeStruct((Z // SLABS, R // GROUPS, A), F32),
        in_specs=[VMEM] * 3,
        out_specs=VMEM,
        scratch_shapes=[pltpu.VMEM((A + 16, Z), F32)],
        compiler_params=PARAMS,
        cost_estimate=cost(1 << 29, 4 << 20),
        name="last",
    )(packed, high, low)


def exchange(packed):
    blocks = packed.reshape(SLABS * GROUPS, 4, Z)
    return lax.all_to_all(blocks, ("slab", "freq"), 0, 0, tiled=True).reshape(packed.shape)


def on_device(initial, measured, projector, offsets):
    (angles, angles_low), (even, _), (odd, _) = tables()
    slab = lax.axis_index("slab").astype(jnp.int32)
    group = lax.axis_index("freq").astype(jnp.int32)
    silent = ((slab == 0) & (group == 0)).astype(jnp.int32).reshape(1)
    slab = slab.reshape(1)
    pieces = list(arrange(slab, initial, measured))
    for distance in range(1, SLABS):
        pairs = [(i, (i + distance) % SLABS) for i in range(SLABS)]
        pieces[distance] = lax.ppermute(pieces[distance], "slab", pairs)
    turned, plain_0, plain_far, offsets = prepare(slab, offsets, projector)
    kept, measured, packed = first_half(slab, offsets, pieces, turned, plain_0, plain_far)
    packed = exchange(middle(exchange(packed), angles, even, odd))
    packed = later_half(slab, silent, offsets, packed, kept, measured, turned, plain_far)
    return last(exchange(packed), angles, angles_low)


def solution(mesh):
    placed = (
        P(None, "freq", "slab", None),
        P(None, "freq", "slab", None),
        P(None, None, "freq", None, None),
        P(),
    )
    return jax.shard_map(
        on_device, mesh=mesh, in_specs=placed, out_specs=P("slab", "freq", None), check_vma=False
    )
```
